512 devices in a mesh: seq: 64 (over z, y), head: 8 (over x, core).
Axes of the slice: x: 4, y: 8, z: 8, core: 2. Of those that a mesh axis runs over, the one named last changes fastest.
Arguments:
- queries: bfloat16 [9216, 8192], P('seq', 'head'), may hold values from -24 to 24
- key_matrix: bfloat16 [9216, 1024], P('seq', 'head'), may hold values from -4 to 4
- value_matrix: bfloat16 [9216, 1024], P('seq', 'head'), may hold values from -6 to 6
- query_feature_weight: bfloat16 [128, 4096], P(None, 'head'), may hold values from -0.5 to 0.5
- key_feature_weight: bfloat16 [128, 512], P(None, 'head'), may hold values from -0.5 to 0.5
Outputs:
- student_out: bfloat16 [9216, 8192], P('seq', 'head')
- query_map_grad: float32 [128, 4096], P(None, 'head')
- key_weight_gradient: float32 [128, 512], P(None, 'head')
- transfer_loss: float32 [], replicated
The draws below stay inside these ranges and needn't reach their ends.
All inputs are finite; a program needn't handle non-finite values.
Results may differ from the reference program's by a relative error of at most 0.008.
Values may be sent and summed in bfloat16 or wider, within the bound.
A program may use at most 128 MiB of HBM per device.

```python
import jax
import jax.numpy as jnp
from jax import lax

HEAD_SIZE = 128
GROUP_QUERIES = 8
HALF_FEATURES = 64
TOK_DEV = 144
KEY_VALUE_HEADS = 8
QUERY_HEADS = 64
SEGMENT_TOKENS = 9216


def query_key_pair(key):
    base_key = jax.random.fold_in(key, 7)
    key_portion, query_part = jax.random.split(base_key)
    key_numbers = jax.random.truncated_normal(key_portion, -4.0, 4.0, (SEGMENT_TOKENS, KEY_VALUE_HEADS * HEAD_SIZE), jnp.float32)
    query_vals = jax.random.truncated_normal(query_part, -4.0, 4.0, (SEGMENT_TOKENS, QUERY_HEADS * HEAD_SIZE), jnp.float32)
    return (query_vals, key_numbers)


def draw_queries(key, part):
    return query_key_pair(key)[0].astype(jnp.bfloat16)


def draw_key_matrix(key, part):
    return query_key_pair(key)[1].astype(jnp.bfloat16)


def level_of(own_key, extent, cuts, low, largest):
    def one(dim, shards_of):
        draws = jax.random.uniform(jax.random.fold_in(jax.random.fold_in(own_key, 6), dim), (shards_of,), jnp.float32, low / len(cuts), largest / len(cuts))
        return jnp.repeat(jnp.exp(draws), extent[dim] // shards_of).reshape((-1,) + (1,) * (len(extent) - dim - 1))

    gain = one(*cuts[0])
    for cut in cuts[1:]:
        gain = gain * one(*cut)
    return gain


def noise(own_key, dims, width, reach, cuts=(), kind=jnp.bfloat16):
    result = jax.random.normal(own_key, dims, jnp.float32) * width
    if len(cuts) > 0:
        result = level_of(own_key, dims, cuts, -0.22, 0.18) * result
    return jnp.clip(result, min=-reach, max=reach).astype(kind)


def setup_inputs(seed: int = 0) -> dict:
    key_list = jax.random.split(jax.random.key(seed), 6)
    queries = draw_queries(jax.random.fold_in(key_list[5], 71), 0)
    key_matrix = draw_key_matrix(jax.random.fold_in(key_list[5], 71), 0)
    value_matrix = noise(key_list[2], (SEGMENT_TOKENS, KEY_VALUE_HEADS * HEAD_SIZE), 1.0, 6.0, ((0, 64), (1, 8)))
    query_feature_weight = noise(key_list[3], (HEAD_SIZE, QUERY_HEADS * HALF_FEATURES), HEAD_SIZE ** -0.5, 0.5, ((1, 8),))
    key_feature_weight = noise(key_list[4], (HEAD_SIZE, KEY_VALUE_HEADS * HALF_FEATURES), HEAD_SIZE ** -0.5, 0.5, ((1, 8),))
    return {"queries": queries, "key_matrix": key_matrix, "value_matrix": value_matrix, "query_feature_weight": query_feature_weight, "key_feature_weight": key_feature_weight}


def rounded(array):
    return lax.optimization_barrier(array.astype(jnp.bfloat16)).astype(jnp.float32)


def feature_pair(logits):
    plus_half = jax.nn.softmax(logits, axis=-1)
    minus_half = jax.nn.softmax(-logits, axis=-1)
    return plus_half, minus_half


def pair_backward(plus_half, minus_half, d_features):
    feat_count = plus_half.shape[-1]
    d_plus = d_features[..., :feat_count]
    d_minus = d_features[..., feat_count:]
    inner_plus = jnp.sum(d_plus * plus_half, axis=-1, keepdims=True)
    inner_minus = jnp.sum(d_minus * minus_half, axis=-1, keepdims=True)
    return plus_half * (d_plus - inner_plus) - minus_half * (d_minus - inner_minus)


def exclusive(array):
    totals = jnp.cumsum(array, axis=0)
    return jnp.concatenate([jnp.zeros_like(array[:1]), totals[:-1]], axis=0)


def teacher_head(query_head, key_head, value_head):
    blocks = SEGMENT_TOKENS // TOK_DEV
    highest = lax.Precision.HIGHEST
    key_wide = key_head.astype(jnp.float32)
    value_wide = value_head.astype(jnp.float32)
    key_pos = jnp.arange(SEGMENT_TOKENS, dtype=jnp.int32)
    query_blocks = query_head.reshape(blocks, TOK_DEV, GROUP_QUERIES, HEAD_SIZE)

    def one_block(inputs):
        row_block, block_index = inputs
        scores = jnp.einsum("tgd,sd->gts", row_block.astype(jnp.float32), key_wide, precision=highest) * (HEAD_SIZE ** -0.5)
        query_pos = block_index * TOK_DEV + jnp.arange(TOK_DEV, dtype=jnp.int32)
        visible = key_pos[None, None, :] <= query_pos[None, :, None]
        masked = jnp.where(visible, scores, -jnp.inf)
        row_max = jnp.max(masked, axis=-1, keepdims=True)
        exponent = jnp.exp(masked - row_max)
        row_sum = jnp.sum(exponent, axis=-1)
        mixed_rows = jnp.einsum("gts,sd->gtd", rounded(exponent), value_wide, precision=highest) / row_sum[..., None]
        return mixed_rows.astype(jnp.bfloat16)

    return lax.map(one_block, (query_blocks, jnp.arange(blocks, dtype=jnp.int32)))


def student_head(query_head, key_head, value_head, query_map_head, key_map_head, teacher_blocks):
    blocks = SEGMENT_TOKENS // TOK_DEV
    highest = lax.Precision.HIGHEST
    query_wide = query_head.astype(jnp.float32)
    key_wide = key_head.astype(jnp.float32)
    value_wide = value_head.astype(jnp.float32).reshape(blocks, TOK_DEV, HEAD_SIZE)
    query_logits = jnp.einsum("sgd,dgf->gsf", query_wide, query_map_head.astype(jnp.float32), precision=highest)
    query_plus, query_minus = feature_pair(query_logits)
    query_phi = rounded(jnp.concatenate([query_plus, query_minus], axis=-1))
    phi_blocks = query_phi.reshape(GROUP_QUERIES, blocks, TOK_DEV, 2 * HALF_FEATURES).transpose(1, 0, 2, 3)
    key_logits = jnp.einsum("sd,df->sf", key_wide, key_map_head.astype(jnp.float32), precision=highest)
    key_plus, key_minus = feature_pair(key_logits)
    key_phi = rounded(jnp.concatenate([key_plus, key_minus], axis=-1)).reshape(blocks, TOK_DEV, 2 * HALF_FEATURES)
    block_state = jnp.einsum("ntf,ntd->nfd", key_phi, value_wide, precision=highest)
    block_norm = jnp.sum(key_phi, axis=1)
    prefix_state = exclusive(block_state)
    prefix_norm = exclusive(block_norm)
    prefix_low = rounded(prefix_state)
    token_index = jnp.arange(TOK_DEV, dtype=jnp.int32)
    causal = token_index[None, :] <= token_index[:, None]
    intra_scores = jnp.where(causal, jnp.einsum("ngtf,nsf->ngts", phi_blocks, key_phi, precision=highest), 0.0)
    numerator = jnp.einsum("ngts,nsd->ngtd", rounded(intra_scores), value_wide, precision=highest)
    numerator = numerator + jnp.einsum("ngtf,nfd->ngtd", phi_blocks, prefix_low, precision=highest)
    denominator = jnp.sum(intra_scores, axis=-1) + jnp.einsum("ngtf,nf->ngt", phi_blocks, prefix_norm, precision=highest)
    student = numerator / denominator[..., None]
    target = teacher_blocks.astype(jnp.float32)
    differ = student - target
    loss_part = jnp.sum(differ * differ)
    grad_out = 2.0 * differ / SEGMENT_TOKENS
    numer_grad = grad_out / denominator[..., None]
    denom_grad = -jnp.sum(grad_out * student, axis=-1) / denominator
    numer_low = rounded(numer_grad)
    coupling = jnp.einsum("ngtd,nsd->ngts", numer_low, value_wide, precision=highest) + denom_grad[..., None]
    coupling_low = rounded(jnp.where(causal, coupling, 0.0))
    later_state = jnp.einsum("ngtf,ngtd->nfd", phi_blocks, numer_low, precision=highest)
    later_norm = jnp.einsum("ngtf,ngt->nf", phi_blocks, denom_grad, precision=highest)
    suffix_low = rounded(exclusive(later_state[::-1])[::-1])
    suffix_norm = exclusive(later_norm[::-1])[::-1]
    query_dphi = jnp.einsum("ngts,nsf->ngtf", coupling_low, key_phi, precision=highest)
    query_dphi = query_dphi + jnp.einsum("ngtd,nfd->ngtf", numer_low, prefix_low, precision=highest)
    query_dphi = query_dphi + denom_grad[..., None] * prefix_norm[:, None, None, :]
    key_dphi = jnp.einsum("ngts,ngtf->nsf", coupling_low, phi_blocks, precision=highest)
    key_dphi = key_dphi + jnp.einsum("nsd,nfd->nsf", value_wide, suffix_low, precision=highest)
    key_dphi = key_dphi + suffix_norm[:, None, :]
    query_dphi_all = query_dphi.transpose(1, 0, 2, 3).reshape(GROUP_QUERIES, SEGMENT_TOKENS, 2 * HALF_FEATURES)
    query_dlogit = rounded(pair_backward(query_plus, query_minus, query_dphi_all))
    key_dlogit = rounded(pair_backward(key_plus, key_minus, key_dphi.reshape(SEGMENT_TOKENS, 2 * HALF_FEATURES)))
    query_grad = jnp.einsum("sgd,gsf->dgf", query_wide, query_dlogit, precision=highest)
    key_grad = jnp.einsum("sd,sf->df", key_wide, key_dlogit, precision=highest)
    student_low = student.astype(jnp.bfloat16).transpose(0, 2, 1, 3).reshape(SEGMENT_TOKENS, GROUP_QUERIES, HEAD_SIZE)
    return student_low, query_grad, key_grad, loss_part


def reference(queries, key_matrix, value_matrix, query_feature_weight, key_feature_weight):
    query_pieces = queries.reshape(SEGMENT_TOKENS, KEY_VALUE_HEADS, GROUP_QUERIES, HEAD_SIZE).transpose(1, 0, 2, 3)
    key_pieces = key_matrix.reshape(SEGMENT_TOKENS, KEY_VALUE_HEADS, HEAD_SIZE).transpose(1, 0, 2)
    value_pieces = value_matrix.reshape(SEGMENT_TOKENS, KEY_VALUE_HEADS, HEAD_SIZE).transpose(1, 0, 2)
    query_weight_pieces = query_feature_weight.reshape(HEAD_SIZE, KEY_VALUE_HEADS, GROUP_QUERIES, HALF_FEATURES).transpose(1, 0, 2, 3)
    key_weight_pieces = key_feature_weight.reshape(HEAD_SIZE, KEY_VALUE_HEADS, HALF_FEATURES).transpose(1, 0, 2)

    def per_head(inputs):
        query_head, key_head, value_head, query_map_head, key_map_head = inputs
        teacher_blocks = teacher_head(query_head, key_head, value_head)
        return student_head(query_head, key_head, value_head, query_map_head, key_map_head, teacher_blocks)

    student_all, query_grads, key_gradient_list, loss_parts = lax.map(per_head, (query_pieces, key_pieces, value_pieces, query_weight_pieces, key_weight_pieces))
    student_out = student_all.transpose(1, 0, 2, 3).reshape(SEGMENT_TOKENS, QUERY_HEADS * HEAD_SIZE)
    query_map_grad = query_grads.transpose(1, 0, 2, 3).reshape(HEAD_SIZE, QUERY_HEADS * HALF_FEATURES)
    key_weight_gradient = key_gradient_list.transpose(1, 0, 2).reshape(HEAD_SIZE, KEY_VALUE_HEADS * HALF_FEATURES)
    transfer_loss = jnp.sum(loss_parts) / SEGMENT_TOKENS
    return student_out, query_map_grad, key_weight_gradient, transfer_loss
```

```python
import functools

import jax
import jax.numpy as jnp
from jax import lax
from jax.experimental import pallas as pl
from jax.experimental.pallas import tpu as pltpu
from jax.sharding import PartitionSpec as P

D = 128
GROUP = 8
HALF = 64
T = 144
SIDE = 8
BLOCKS = SIDE * SIDE
TOKENS = BLOCKS * T
CHUNK = SIDE * T
ROWS = GROUP * T
PAIR = 2 * T
TILES = ROWS // PAIR
NEG = -1e30
SCALE2 = (D ** -0.5) * 1.4426950408889634
MESH = pl.DeviceIdType.MESH
F32 = jnp.float32
BF16 = jnp.bfloat16


def dot(a, b):
    return lax.dot_general(a, b, (((1,), (0,)), ((), ())), preferred_element_type=F32)


def dot_nt(a, b):
    return lax.dot_general(a, b, (((1,), (1,)), ((), ())), preferred_element_type=F32)


def dot_tn(a, b):
    return lax.dot_general(a, b, (((0,), (0,)), ((), ())), preferred_element_type=F32)


def lanes(rows):
    return lax.broadcasted_iota(jnp.int32, (rows, D), 1)


def halves(x, reduce, neutral):
    plus = lanes(x.shape[0]) < HALF
    a = reduce(jnp.where(plus, x, neutral), axis=1, keepdims=True)
    b = reduce(jnp.where(plus, neutral, x), axis=1, keepdims=True)
    return a, b, plus


def feature_pair(x):
    a, b, plus = halves(x, jnp.max, -jnp.inf)
    e = jnp.exp(x - jnp.where(plus, a, b))
    sa, sb, _ = halves(e, jnp.sum, 0.0)
    return e * jnp.where(plus, 1.0 / sa, 1.0 / sb)


def pair_backward(pn, d):
    a, b, plus = halves(pn * d, jnp.sum, 0.0)
    t = pn * (d - jnp.where(plus, a, b))
    return t - pltpu.roll(t, HALF, 1)


def hi_lo(x):
    hi = x.astype(BF16).astype(F32)
    return hi, x - hi


def place():
    seq = lax.axis_index("seq")
    head = lax.axis_index("head")
    core = head % 2
    y, z = seq % SIDE, seq // SIDE
    f = y + core * (z - y)
    s = z + core * (y - z)
    stride_f = 1 + (SIDE - 1) * core
    stride_s = SIDE - (SIDE - 1) * core
    return seq, head, f, s, stride_f, stride_s


def offset(k):
    return k // 2 - (k % 2) * k


def main_kernel(
    q_ref, k_hbm, v_hbm, wq_ref, wk_ref,
    student_ref, qg_ref, kg_ref, loss_ref,
    kv, qs, qpn, kpn, run_max, acc, prefix, later, low, own_dphi, wk2, loss_acc,
    local_sem, recv_sem, f_sem, s_sem,
):
    seq, head, f, s, stride_f, stride_s = place()

    def rank(ff, ss):
        return (ff * stride_f + ss * stride_s, head)

    f_up, f_dn = rank((f + 1) % SIDE, s), rank((f + SIDE - 1) % SIDE, s)
    s_up, s_dn = rank(f, (s + 1) % SIDE), rank(f, (s + SIDE - 1) % SIDE)

    own = s * SIDE + f
    load_k = pltpu.make_async_copy(k_hbm, kv.at[own, pl.ds(0, T)], local_sem.at[0])
    load_v = pltpu.make_async_copy(v_hbm, kv.at[own, pl.ds(T, T)], local_sem.at[1])
    load_k.start()
    load_v.start()
    barrier = pltpu.get_barrier_semaphore()
    for peer in (f_up, f_dn, s_up, s_dn):
        pl.semaphore_signal(barrier, inc=1, device_id=peer, device_id_type=MESH)
    load_k.wait()
    load_v.wait()
    pl.semaphore_wait(barrier, 4)

    def slot_of(ss, ff):
        return ((ss + 2 * SIDE) % SIDE) * SIDE + (ff + 2 * SIDE) % SIDE

    def copy(slot, sem, peer):
        return pltpu.make_async_remote_copy(
            src_ref=kv.at[slot], dst_ref=kv.at[slot], send_sem=sem, recv_sem=recv_sem.at[slot],
            device_id=peer, device_id_type=MESH,
        )

    def f_copy(slot, way):
        return copy(slot, f_sem.at[way, slot % SIDE], (f_up, f_dn)[way])

    def s_copy(slot, way):
        return copy(slot, s_sem.at[way, slot], (s_up, s_dn)[way])

    def arrived(slot):
        f_copy(slot, 0).wait_recv()

    def spread(slot):
        s_copy(slot, 0).start()
        s_copy(slot, 1).start()

    f_copy(own, 0).start()
    f_copy(own, 1).start()
    spread(own)

    wk = wk_ref[...].astype(F32)
    wk2[...] = jnp.concatenate([wk, -wk], axis=1).astype(BF16)
    k_own = kv[own, pl.ds(0, T), :]
    v_own = kv[own, pl.ds(T, T), :]
    pn_own = feature_pair(dot(k_own, wk2[...]))
    kphi_own = pn_own.astype(BF16)
    ones_t = jnp.ones((T, D), BF16)

    row_token = lax.broadcasted_iota(jnp.int32, (PAIR, T), 0)
    row_token = jnp.where(row_token >= T, row_token - T, row_token)
    causal = lax.broadcasted_iota(jnp.int32, (PAIR, T), 1) <= row_token

    prefix[...] = jnp.zeros_like(prefix)
    later[...] = jnp.zeros_like(later)
    own_dphi[...] = jnp.zeros_like(own_dphi)
    loss_acc[...] = jnp.zeros_like(loss_acc)

    def first(j, carry):
        rows = pl.ds(pl.multiple_of(j * PAIR, PAIR), PAIR)
        q_a = q_ref[:, pl.ds(pl.multiple_of(j * 2 * D, D), D)]
        q_b = q_ref[:, pl.ds(pl.multiple_of(j * 2 * D + D, D), D)]
        q = jnp.concatenate([q_a, q_b], axis=0)
        qs[rows, :] = q
        w = wq_ref[:, pl.ds(pl.multiple_of(j * D, D), D)]
        la, lb = dot(q_a, w), dot(q_b, w)
        plus = lanes(T) < HALF
        xa = jnp.where(plus, la, -pltpu.roll(la, HALF, 1))
        xb = jnp.where(plus, pltpu.roll(lb, HALF, 1), -lb)
        qpn[rows, :] = feature_pair(jnp.concatenate([xa, xb], axis=0))
        scores = jnp.where(causal, dot_nt(q, k_own) * SCALE2, NEG)
        top = jnp.max(scores, axis=1, keepdims=True)
        p = jnp.exp2(scores - top).astype(BF16)
        run_max[rows, :] = jnp.broadcast_to(top, (PAIR, D))
        acc[rows, :] = dot(p, jnp.concatenate([v_own, ones_t], axis=1))

        up = slot_of(s, f - j - 1)
        arrived(up)

        @pl.when(j < 3)
        def _():
            f_copy(up, 0).start()

        spread(up)

        @pl.when(j < 3)
        def _():
            dn = slot_of(s, f + j + 1)
            arrived(dn)

            @pl.when(j < 2)
            def _():
                f_copy(dn, 1).start()

            spread(dn)

        return carry

    lax.fori_loop(0, TILES, first, 0)

    def visible(ss, shape, dim):
        block = lax.broadcasted_iota(jnp.int32, shape, dim) // T
        return ss * stride_s + block * stride_f < seq

    def any_visible(ss):
        return ss * stride_s < seq

    def chunk_kv(ss):
        base = pl.multiple_of(ss * SIDE, SIDE)
        k = kv[pl.ds(base, SIDE), pl.ds(0, T), :].reshape(CHUNK, D)
        v = kv[pl.ds(base, SIDE), pl.ds(T, T), :].reshape(CHUNK, D)
        return k, v

    def step(t, carry):
        @pl.when(t < 24)
        def _():
            h, k = t // 8 + 1, t % 8
            ff = f + offset(k)
            up, dn = slot_of(s - h, ff), slot_of(s + h, ff)
            arrived(up)

            @pl.when(h * 8 + k < 28)
            def _():
                s_copy(up, 0).start()

            arrived(dn)

            @pl.when((h < 3) | (k >= 4))
            def _():
                s_copy(dn, 1).start()

        @pl.when(t == 32)
        def _():
            def last(k, carry):
                arrived(slot_of(s - 4, f + offset(k)))
                return carry

            lax.fori_loop(0, 8, last, 0)

        u = t - 4
        ci, tile = u // 4, u % 4
        ss = (s + offset(ci) + 2 * SIDE) % SIDE

        @pl.when((u >= 0) & any_visible(ss))
        def _():
            k, v = chunk_kv(ss)
            v1 = jnp.concatenate([v, jnp.ones((CHUNK, D), BF16)], axis=1)

            @pl.when(tile == 0)
            def _():
                pn = feature_pair(dot(k, wk2[...]))
                pn = jnp.where(visible(ss, (CHUNK, D), 0), pn, 0.0)
                kpn[pl.ds(pl.multiple_of(ss * CHUNK, CHUNK), CHUNK), :] = pn
                prefix[...] += dot_tn(pn.astype(BF16), v1)

            rows = pl.ds(pl.multiple_of(tile * PAIR, PAIR), PAIR)
            bias = jnp.where(visible(ss, (1, CHUNK), 1), 0.0, NEG)
            scores = dot_nt(qs[rows, :], k) * SCALE2 + bias
            old = run_max[rows, :]
            new = jnp.maximum(old, jnp.max(scores, axis=1, keepdims=True))
            p = jnp.exp2(scores - new[:, :1]).astype(BF16)
            alpha = jnp.exp2(old - new)
            run_max[rows, :] = new
            acc[rows, :] = acc[rows, :] * jnp.concatenate([alpha, alpha], axis=1) + dot(p, v1)

        return carry

    lax.fori_loop(0, 36, step, 0)

    lane_d = lanes(D)
    norm_hi, norm_lo = hi_lo(prefix[:, D:])
    low[...] = jnp.concatenate(
        [prefix[:, :D], jnp.where(lane_d < HALF, norm_hi, norm_lo)], axis=1
    ).astype(BF16)
    lane = lanes(PAIR)
    lane_t = lanes(T)
    pick_t = jnp.where((lane_t == 0) | (lane_t == HALF), 1.0, 0.0).astype(BF16)
    v_pick = jnp.concatenate([v_own, pick_t], axis=1)

    def finish(j, carry):
        rows = pl.ds(pl.multiple_of(j * PAIR, PAIR), PAIR)
        pn = qpn[rows, :]
        phi = pn.astype(BF16)
        intra = jnp.where(causal, dot_nt(phi, kphi_own), 0.0)
        far = dot(phi, low[...])
        numer = dot(intra.astype(BF16), v_own) + far[:, :D]
        far_d = far[:, D:]
        denom = jnp.sum(intra, axis=1, keepdims=True) + (far_d + pltpu.roll(far_d, HALF, 1))
        inv = 1.0 / denom
        student = numer * inv
        student_low = student.astype(BF16)
        student_ref[:, pl.ds(pl.multiple_of(j * 2 * D, D), D)] = student_low[:T]
        student_ref[:, pl.ds(pl.multiple_of(j * 2 * D + D, D), D)] = student_low[T:]
        a = acc[rows, :]
        teacher = (a[:, :D] / a[:, D:]).astype(BF16).astype(F32)
        differ = student - teacher
        loss_acc[...] += jnp.sum((differ * differ).reshape(PAIR // 8, 8, D), axis=0)
        grad = differ * (2.0 / TOKENS)
        numer_low = (grad * inv).astype(BF16)
        dg = -jnp.sum(grad * student, axis=1, keepdims=True) * inv
        dg_hi, dg_lo = hi_lo(dg)
        zero = jnp.zeros_like(dg)
        g_key = jnp.where(lane == 0, dg_hi, jnp.where(lane == HALF, dg_lo, zero)).astype(BF16)
        g_later = jnp.where(lane < HALF, dg_hi, dg_lo).astype(BF16)
        g_norm = jnp.where(
            (lane == 0) | (lane == HALF), dg_hi, jnp.where(lane == 1, dg_lo, zero)
        ).astype(BF16)
        coupling = dot_nt(jnp.concatenate([numer_low, g_key], axis=1), v_pick)
        coupling = jnp.where(causal, coupling, 0.0).astype(BF16)
        later[...] += dot_tn(phi, jnp.concatenate([numer_low, g_later], axis=1))
        own_dphi[...] += dot_tn(coupling, phi)
        dphi = dot(coupling, kphi_own)
        dphi = dphi + dot_nt(jnp.concatenate([numer_low, g_norm], axis=1), low[...])
        dl = pair_backward(pn, dphi).astype(BF16)
        q = qs[rows, :]
        ga, gb = dot_tn(q[:T], dl[:T]), dot_tn(q[T:], dl[T:])
        qg_ref[:, pl.ds(pl.multiple_of(j * D, D), D)] = jnp.where(lane_d < HALF, ga, -gb)
        return carry

    lax.fori_loop(0, TILES, finish, 0)

    norm = later[:, D:]
    norm_hi, norm_lo = hi_lo(norm + pltpu.roll(norm, HALF, 1))
    low[...] = jnp.concatenate(
        [later[:, :D], jnp.where(lane_d < HALF, norm_hi, norm_lo)], axis=1
    ).astype(BF16)
    dl_own = pair_backward(pn_own, own_dphi[...]).astype(BF16)
    kg_ref[...] = dot_tn(k_own, dl_own)
    lane_c = lanes(CHUNK)
    pick_c = jnp.where((lane_c == 0) | (lane_c == HALF), 1.0, 0.0).astype(BF16)

    def back(ss, carry):
        @pl.when(any_visible(ss))
        def _():
            k, v = chunk_kv(ss)
            d = dot_nt(jnp.concatenate([v, pick_c], axis=1), low[...])
            pn = kpn[pl.ds(pl.multiple_of(ss * CHUNK, CHUNK), CHUNK), :]
            kg_ref[...] += dot_tn(k, pair_backward(pn, d).astype(BF16))

        return carry

    lax.fori_loop(0, SIDE, back, 0)
    loss_ref[...] = loss_acc[...]

    def drain_f(j, carry):
        @pl.when(j < 4)
        def _():
            f_copy(slot_of(s, f - j), 0).wait_send()

        @pl.when(j < 3)
        def _():
            f_copy(slot_of(s, f + j), 1).wait_send()

        return carry

    lax.fori_loop(0, 4, drain_f, 0)

    def drain_s(t, carry):
        h, k = t // 8, t % 8
        ff = f + offset(k)

        @pl.when(t < 28)
        def _():
            s_copy(slot_of(s - h, ff), 0).wait_send()

        @pl.when((h < 3) | (k >= 4))
        def _():
            s_copy(slot_of(s + h, ff), 1).wait_send()

        return carry

    lax.fori_loop(0, 32, drain_s, 0)


ORDER = (4, 3, 5, 2, 6, 1, 7)
WIDE = 640


def reduce_kernel(
    qg_ref, kg_ref, loss_ref, qo_ref, ko_ref, lo_ref,
    parts, got1, mid, got2, full, got3, mine, got_loss,
    send1, recv1, send2, recv2, send3, recv3, send4, recv4,
):
    seq, head, f, s, stride_f, stride_s = place()

    def f_rank(j):
        return (((f + j) % SIDE) * stride_f + s * stride_s, head)

    def s_rank(j):
        return (f * stride_f + ((s + j) % SIDE) * stride_s, head)

    def h_rank(j):
        return (seq, (head + j) % SIDE)

    barrier = pltpu.get_barrier_semaphore()
    for rank in (f_rank, s_rank, h_rank):
        for j in range(1, SIDE):
            pl.semaphore_signal(barrier, inc=1, device_id=rank(j), device_id_type=MESH)

    loss = jnp.sum(loss_ref[...], keepdims=True).reshape(1, 1)
    loss_hi, loss_lo = hi_lo(loss)
    lane = lanes(16)
    row = lax.broadcasted_iota(jnp.int32, (16, D), 0)
    extra = jnp.where(row == 0, loss_hi, jnp.where(row == 1, loss_lo, 0.0))
    for i in range(SIDE):
        parts[i, :, pl.ds(0, 512)] = qg_ref[pl.ds(16 * i, 16), :].astype(BF16)
        k = kg_ref[pl.ds(16 * i, 16), :]
        parts[i, :, pl.ds(512, D)] = jnp.where(lane < HALF, k, extra).astype(BF16)
    pl.semaphore_wait(barrier, 3 * (SIDE - 1))

    def copies(src, dst, me, send, recv, rank):
        def make(j):
            return pltpu.make_async_remote_copy(
                src_ref=src(j), dst_ref=dst.at[me], send_sem=send.at[j], recv_sem=recv.at[me],
                device_id=rank(j), device_id_type=MESH,
            )

        def arrival(j):
            slot = (me + j) % SIDE
            return pltpu.make_async_remote_copy(
                src_ref=src(j), dst_ref=dst.at[slot], send_sem=send.at[j], recv_sem=recv.at[slot],
                device_id=rank(j), device_id_type=MESH,
            )

        return make, arrival

    make1, arrive1 = copies(lambda j: parts.at[(f + j) % SIDE], got1, f, send1, recv1, f_rank)
    for j in ORDER:
        make1(j).start()
    total = parts[f].astype(F32)
    for j in range(1, SIDE):
        arrive1(j).wait_recv()
        total = total + got1[(f + j) % SIDE].astype(F32)

    def split(total):
        tail = total[:, 512:]
        value = tail[0:1, HALF:HALF + 1] + tail[1:2, HALF:HALF + 1]
        return tail, value

    def pack(total):
        tail, value = split(total)
        hi, lo = hi_lo(value)
        tail = jnp.where(lane < HALF, tail, jnp.where(row == 0, hi, jnp.where(row == 1, lo, 0.0)))
        return jnp.concatenate([total[:, :512], tail], axis=1).astype(BF16)

    mid[...] = pack(total)
    make2, arrive2 = copies(lambda j: mid, got2, s, send2, recv2, s_rank)
    for j in ORDER:
        make2(j).start()
    total = mid[...].astype(F32)
    for j in range(1, SIDE):
        arrive2(j).wait_recv()
        total = total + got2[(s + j) % SIDE].astype(F32)

    full[...] = total.astype(BF16)
    make3, arrive3 = copies(lambda j: full, got3, f, send3, recv3, f_rank)
    for j in ORDER:
        make3(j).start()
    _, value = split(total)
    mine[...] = jnp.broadcast_to(value, (8, D))
    make4, arrive4 = copies(lambda j: mine, got_loss, head, send4, recv4, h_rank)
    for j in range(1, SIDE):
        make4(j).start()

    def put(i, block):
        rows = pl.ds(pl.multiple_of(i * 16, 16), 16)
        qo_ref[rows, :] = block[:, :512]
        ko_ref[rows, :] = block[:, 512:512 + HALF]

    put(f, total)
    for j in range(1, SIDE):
        arrive3(j).wait_recv()
        slot = (f + j) % SIDE
        put(slot, got3[slot].astype(F32))
    value = mine[...]
    for j in range(1, SIDE):
        arrive4(j).wait_recv()
        value = value + got_loss[(head + j) % SIDE]
    lo_ref[...] = value * (1.0 / TOKENS)
    for make in (make1, make2, make3, make4):
        for j in range(1, SIDE):
            make(j).wait_send()


def local(queries, key_matrix, value_matrix, query_feature_weight, key_feature_weight):
    vmem = pl.BlockSpec(memory_space=pltpu.VMEM)
    anywhere = pl.BlockSpec(memory_space=pl.ANY)
    dma = pltpu.SemaphoreType.DMA
    student, qg, kg, loss = pl.pallas_call(
        main_kernel,
        out_shape=(
            jax.ShapeDtypeStruct((T, GROUP * D), BF16),
            jax.ShapeDtypeStruct((D, GROUP * HALF), F32),
            jax.ShapeDtypeStruct((D, D), F32),
            jax.ShapeDtypeStruct((8, D), F32),
        ),
        in_specs=[vmem, anywhere, anywhere, vmem, vmem],
        out_specs=(vmem, vmem, vmem, vmem),
        scratch_shapes=[
            pltpu.VMEM((BLOCKS, 2 * T, D), BF16),
            pltpu.VMEM((ROWS, D), BF16),
            pltpu.VMEM((ROWS, D), F32),
            pltpu.VMEM((TOKENS, D), F32),
            pltpu.VMEM((ROWS, D), F32),
            pltpu.VMEM((ROWS, 2 * D), F32),
            pltpu.VMEM((D, 2 * D), F32),
            pltpu.VMEM((D, 2 * D), F32),
            pltpu.VMEM((D, 2 * D), BF16),
            pltpu.VMEM((T, D), F32),
            pltpu.VMEM((D, D), BF16),
            pltpu.VMEM((8, D), F32),
            dma((2,)),
            dma((BLOCKS,)),
            dma((2, SIDE)),
            dma((2, BLOCKS)),
        ],
        compiler_params=pltpu.CompilerParams(
            collective_id=0, has_side_effects=True, vmem_limit_bytes=56 * 1024 * 1024
        ),
        name="attend",
    )(queries, key_matrix, value_matrix, query_feature_weight, key_feature_weight)
    qo, ko, lo = pl.pallas_call(
        reduce_kernel,
        out_shape=(
            jax.ShapeDtypeStruct((D, GROUP * HALF), F32),
            jax.ShapeDtypeStruct((D, HALF), F32),
            jax.ShapeDtypeStruct((8, D), F32),
        ),
        in_specs=[vmem] * 3,
        out_specs=(vmem,) * 3,
        scratch_shapes=[
            pltpu.VMEM((SIDE, 16, WIDE), BF16),
            pltpu.VMEM((SIDE, 16, WIDE), BF16),
            pltpu.VMEM((16, WIDE), BF16),
            pltpu.VMEM((SIDE, 16, WIDE), BF16),
            pltpu.VMEM((16, WIDE), BF16),
            pltpu.VMEM((SIDE, 16, WIDE), BF16),
            pltpu.VMEM((8, D), F32),
            pltpu.VMEM((SIDE, 8, D), F32),
        ]
        + [dma((SIDE,))] * 8,
        compiler_params=pltpu.CompilerParams(collective_id=1, has_side_effects=True),
        name="combine",
    )(qg, kg, loss)
    return student, qo, ko, lo[0, 0]


def solution(mesh):
    placed = (
        P("seq", "head"),
        P("seq", "head"),
        P("seq", "head"),
        P(None, "head"),
        P(None, "head"),
    )
    return jax.shard_map(
        local,
        mesh=mesh,
        in_specs=placed,
        out_specs=(P("seq", "head"), P(None, "head"), P(None, "head"), P()),
        check_vma=False,
    )
```

```python
import functools

import jax
import jax.numpy as jnp
from jax import lax
from jax.experimental import pallas as pl
from jax.experimental.pallas import tpu as pltpu
from jax.sharding import PartitionSpec as P

D = 128
GROUP = 8
HALF = 64
T = 144
SIDE = 8
BLOCKS = SIDE * SIDE
TOKENS = BLOCKS * T
CHUNK = SIDE * T
ROWS = GROUP * T
PAIR = 2 * T
TILES = ROWS // PAIR
NEG = -1e30
SCALE2 = (D ** -0.5) * 1.4426950408889634
MESH = pl.DeviceIdType.MESH
F32 = jnp.float32
BF16 = jnp.bfloat16


def dot(a, b):
    return lax.dot_general(a, b, (((1,), (0,)), ((), ())), preferred_element_type=F32)


def dot_nt(a, b):
    return lax.dot_general(a, b, (((1,), (1,)), ((), ())), preferred_element_type=F32)


def dot_tn(a, b):
    return lax.dot_general(a, b, (((0,), (0,)), ((), ())), preferred_element_type=F32)


def lanes(rows):
    return lax.broadcasted_iota(jnp.int32, (rows, D), 1)


def halves(x, reduce, neutral):
    plus = lanes(x.shape[0]) < HALF
    a = reduce(jnp.where(plus, x, neutral), axis=1, keepdims=True)
    b = reduce(jnp.where(plus, neutral, x), axis=1, keepdims=True)
    return a, b, plus


def feature_pair(x):
    a, b, plus = halves(x, jnp.max, -jnp.inf)
    e = jnp.exp(x - jnp.where(plus, a, b))
    sa, sb, _ = halves(e, jnp.sum, 0.0)
    return e * jnp.where(plus, 1.0 / sa, 1.0 / sb)


def pair_backward(pn, d):
    a, b, plus = halves(pn * d, jnp.sum, 0.0)
    t = pn * (d - jnp.where(plus, a, b))
    return t - pltpu.roll(t, HALF, 1)


def feature_pair_t(x):
    a = jnp.max(x, axis=0, keepdims=True)
    b = jnp.min(x, axis=0, keepdims=True)
    e, g = jnp.exp(x - a), jnp.exp(b - x)
    e = e * (1.0 / jnp.sum(e, axis=0, keepdims=True))
    g = g * (1.0 / jnp.sum(g, axis=0, keepdims=True))
    return e, g


def pair_backward_t(e, g, d):
    dp, dn = d[:HALF], d[HALF:]
    a = jnp.sum(e * dp, axis=0, keepdims=True)
    b = jnp.sum(g * dn, axis=0, keepdims=True)
    return e * (dp - a) - g * (dn - b)


def hi_lo(x):
    hi = x.astype(BF16).astype(F32)
    return hi, x - hi


def place():
    seq = lax.axis_index("seq")
    head = lax.axis_index("head")
    core = head % 2
    y, z = seq % SIDE, seq // SIDE
    f = y + core * (z - y)
    s = z + core * (y - z)
    stride_f = 1 + (SIDE - 1) * core
    stride_s = SIDE - (SIDE - 1) * core
    return seq, head, f, s, stride_f, stride_s


def offset(k):
    return k // 2 - (k % 2) * k


def main_kernel(
    q_ref, k_hbm, v_hbm, wq_ref, wk_ref,
    student_ref, qg_ref, kg_ref, loss_ref,
    kv, qs, qpn, kpn, run_max, acc, scores, probs, prefix, later, low, own_dphi, wkt, loss_acc,
    local_sem, recv_sem, f_sem, s_sem,
):
    seq, head, f, s, stride_f, stride_s = place()

    def rank(ff, ss):
        return (ff * stride_f + ss * stride_s, head)

    f_up, f_dn = rank((f + 1) % SIDE, s), rank((f + SIDE - 1) % SIDE, s)
    s_up, s_dn = rank(f, (s + 1) % SIDE), rank(f, (s + SIDE - 1) % SIDE)

    own = s * SIDE + f
    load_k = pltpu.make_async_copy(k_hbm, kv.at[own, pl.ds(0, T)], local_sem.at[0])
    load_v = pltpu.make_async_copy(v_hbm, kv.at[own, pl.ds(T, T)], local_sem.at[1])
    load_k.start()
    load_v.start()
    barrier = pltpu.get_barrier_semaphore()
    for peer in (f_up, f_dn, s_up, s_dn):
        pl.semaphore_signal(barrier, inc=1, device_id=peer, device_id_type=MESH)
    load_k.wait()
    load_v.wait()
    pl.semaphore_wait(barrier, 4)

    def slot_of(ss, ff):
        return ((ss + 2 * SIDE) % SIDE) * SIDE + (ff + 2 * SIDE) % SIDE

    def copy(slot, sem, peer):
        return pltpu.make_async_remote_copy(
            src_ref=kv.at[slot], dst_ref=kv.at[slot], send_sem=sem, recv_sem=recv_sem.at[slot],
            device_id=peer, device_id_type=MESH,
        )

    def f_copy(slot, way):
        return copy(slot, f_sem.at[way, slot % SIDE], (f_up, f_dn)[way])

    def s_copy(slot, way):
        return copy(slot, s_sem.at[way, slot], (s_up, s_dn)[way])

    def arrived(slot):
        f_copy(slot, 0).wait_recv()

    def spread(slot):
        s_copy(slot, 0).start()
        s_copy(slot, 1).start()

    f_copy(own, 0).start()
    f_copy(own, 1).start()
    spread(own)

    wkt[...] = wk_ref[...].astype(F32).T.astype(BF16)
    k_own = kv[own, pl.ds(0, T), :]
    v_own = kv[own, pl.ds(T, T), :]
    e_own, g_own = feature_pair_t(dot_nt(wkt[...], k_own))
    kphi_own = jnp.concatenate([e_own, g_own], axis=0).astype(BF16)
    ones_t = jnp.ones((T, D), BF16)

    row_token = lax.broadcasted_iota(jnp.int32, (PAIR, T), 0)
    row_token = jnp.where(row_token >= T, row_token - T, row_token)
    causal = lax.broadcasted_iota(jnp.int32, (PAIR, T), 1) <= row_token

    prefix[...] = jnp.zeros_like(prefix)
    later[...] = jnp.zeros_like(later)
    own_dphi[...] = jnp.zeros_like(own_dphi)
    loss_acc[...] = jnp.zeros_like(loss_acc)

    def first(j, carry):
        rows = pl.ds(pl.multiple_of(j * PAIR, PAIR), PAIR)
        q_a = q_ref[:, pl.ds(pl.multiple_of(j * 2 * D, D), D)]
        q_b = q_ref[:, pl.ds(pl.multiple_of(j * 2 * D + D, D), D)]
        q = jnp.concatenate([q_a, q_b], axis=0)
        qs[rows, :] = q
        w = wq_ref[:, pl.ds(pl.multiple_of(j * D, D), D)]
        la, lb = dot(q_a, w), dot(q_b, w)
        plus = lanes(T) < HALF
        xa = jnp.where(plus, la, -pltpu.roll(la, HALF, 1))
        xb = jnp.where(plus, pltpu.roll(lb, HALF, 1), -lb)
        qpn[rows, :] = feature_pair(jnp.concatenate([xa, xb], axis=0))
        scores = jnp.where(causal, dot_nt(q, k_own) * SCALE2, NEG)
        top = jnp.max(scores, axis=1, keepdims=True)
        p = jnp.exp2(scores - top).astype(BF16)
        run_max[rows, :] = jnp.broadcast_to(top, (PAIR, D))
        acc[rows, :] = dot(p, jnp.concatenate([v_own, ones_t], axis=1))

        up = slot_of(s, f - j - 1)
        arrived(up)

        @pl.when(j < 3)
        def _():
            f_copy(up, 0).start()

        spread(up)

        @pl.when(j < 3)
        def _():
            dn = slot_of(s, f + j + 1)
            arrived(dn)

            @pl.when(j < 2)
            def _():
                f_copy(dn, 1).start()

            spread(dn)

        return carry

    lax.fori_loop(0, TILES, first, 0)

    def visible(ss):
        block = lax.broadcasted_iota(jnp.int32, (1, CHUNK), 1) // T
        return ss * stride_s + block * stride_f < seq

    def any_visible(ss):
        return ss * stride_s < seq

    def chunk_kv(ss):
        base = pl.multiple_of(ss * SIDE, SIDE)
        k = kv[pl.ds(base, SIDE), pl.ds(0, T), :].reshape(CHUNK, D)
        v = kv[pl.ds(base, SIDE), pl.ds(T, T), :].reshape(CHUNK, D)
        return k, v

    def relay(n, carry):
        h, k = n // 8 + 1, n % 8
        ff = f + offset(k)
        up, dn = slot_of(s - h, ff), slot_of(s + h, ff)
        arrived(up)

        @pl.when(n < 20)
        def _():
            s_copy(up, 0).start()

        arrived(dn)

        @pl.when((h < 3) | (k >= 4))
        def _():
            s_copy(dn, 1).start()

        return carry

    def last(k, carry):
        arrived(slot_of(s - 4, f + offset(k)))
        return carry

    def step(ci, carry):
        @pl.when(ci < 6)
        def _():
            lax.fori_loop(4 * ci, 4 * ci + 4, relay, 0)

        @pl.when(ci == 7)
        def _():
            lax.fori_loop(0, 8, last, 0)

        ss = (s + offset(ci) + 2 * SIDE) % SIDE

        @pl.when(any_visible(ss))
        def _():
            k, v = chunk_kv(ss)
            v1 = jnp.concatenate([v, jnp.ones((CHUNK, D), BF16)], axis=1)
            seen = visible(ss)
            bias = jnp.where(seen, 0.0, NEG)
            cuts = [(i, min(256, CHUNK - i)) for i in range(0, CHUNK, 256)]

            def score(r):
                rows = pl.ds(r * PAIR, PAIR)
                q = qs[rows, :]
                top = None
                for i, n in cuts:
                    x = dot_nt(q, k[i:i + n]) * SCALE2 + bias[:, i:i + n]
                    scores[r % 2, :, pl.ds(i, n)] = x
                    for c in range(0, n, D):
                        top = x[:, c:c + D] if top is None else jnp.maximum(top, x[:, c:c + D])
                old = run_max[rows, :]
                new = jnp.maximum(old, jnp.max(top, axis=1, keepdims=True))
                run_max[rows, :] = new
                return new, jnp.exp2(old - new)

            def weigh(r, new, alpha):
                rows = pl.ds(r * PAIR, PAIR)
                for i in range(0, CHUNK, D):
                    x = scores[r % 2, :, pl.ds(i, D)]
                    probs[r % 2, :, pl.ds(i, D)] = jnp.exp2(x - new).astype(BF16)
                out = dot(probs[r % 2], v1)
                acc[rows, :] = acc[rows, :] * jnp.concatenate([alpha, alpha], axis=1) + out

            held = score(0)
            e, g = feature_pair_t(dot_nt(wkt[...], k))
            pn = jnp.where(seen, jnp.concatenate([e, g], axis=0), 0.0)
            kpn[ss] = pn
            prefix[...] += dot(pn.astype(BF16), v1)
            for r in range(TILES):
                ahead = score(r + 1) if r + 1 < TILES else None
                weigh(r, *held)
                held = ahead

        return carry

    lax.fori_loop(0, SIDE, step, 0)

    lane_d = lanes(D)
    norm_hi, norm_lo = hi_lo(prefix[:, D:])
    low[...] = jnp.concatenate(
        [prefix[:, :D], jnp.where(lane_d < HALF, norm_hi, norm_lo)], axis=1
    ).astype(BF16)
    lane = lanes(PAIR)
    lane_t = lanes(T)
    pick_t = jnp.where((lane_t == 0) | (lane_t == HALF), 1.0, 0.0).astype(BF16)
    v_pick = jnp.concatenate([v_own, pick_t], axis=1)

    def finish(j, carry):
        rows = pl.ds(pl.multiple_of(j * PAIR, PAIR), PAIR)
        pn = qpn[rows, :]
        phi = pn.astype(BF16)
        intra = jnp.where(causal, dot(phi, kphi_own), 0.0)
        far = dot(phi, low[...])
        numer = dot(intra.astype(BF16), v_own) + far[:, :D]
        far_d = far[:, D:]
        denom = jnp.sum(intra, axis=1, keepdims=True) + (far_d + pltpu.roll(far_d, HALF, 1))
        inv = 1.0 / denom
        student = numer * inv
        student_low = student.astype(BF16)
        student_ref[:, pl.ds(pl.multiple_of(j * 2 * D, D), D)] = student_low[:T]
        student_ref[:, pl.ds(pl.multiple_of(j * 2 * D + D, D), D)] = student_low[T:]
        a = acc[rows, :]
        teacher = (a[:, :D] / a[:, D:]).astype(BF16).astype(F32)
        differ = student - teacher
        loss_acc[...] += jnp.sum((differ * differ).reshape(PAIR // 8, 8, D), axis=0)
        grad = differ * (2.0 / TOKENS)
        numer_low = (grad * inv).astype(BF16)
        dg = -jnp.sum(grad * student, axis=1, keepdims=True) * inv
        dg_hi, dg_lo = hi_lo(dg)
        zero = jnp.zeros_like(dg)
        g_key = jnp.where(lane == 0, dg_hi, jnp.where(lane == HALF, dg_lo, zero)).astype(BF16)
        g_later = jnp.where(lane < HALF, dg_hi, dg_lo).astype(BF16)
        g_norm = jnp.where(
            (lane == 0) | (lane == HALF), dg_hi, jnp.where(lane == 1, dg_lo, zero)
        ).astype(BF16)
        coupling = dot_nt(jnp.concatenate([numer_low, g_key], axis=1), v_pick)
        coupling = jnp.where(causal, coupling, 0.0).astype(BF16)
        later[...] += dot_tn(phi, jnp.concatenate([numer_low, g_later], axis=1))
        own_dphi[...] += dot_tn(phi, coupling)
        dphi = dot_nt(coupling, kphi_own)
        dphi = dphi + dot_nt(jnp.concatenate([numer_low, g_norm], axis=1), low[...])
        dl = pair_backward(pn, dphi).astype(BF16)
        q = qs[rows, :]
        ga, gb = dot_tn(q[:T], dl[:T]), dot_tn(q[T:], dl[T:])
        qg_ref[:, pl.ds(pl.multiple_of(j * D, D), D)] = jnp.where(lane_d < HALF, ga, -gb)
        return carry

    lax.fori_loop(0, TILES, finish, 0)

    norm = later[:, D:]
    norm_hi, norm_lo = hi_lo(norm + pltpu.roll(norm, HALF, 1))
    low[...] = jnp.concatenate(
        [later[:, :D], jnp.where(lane_d < HALF, norm_hi, norm_lo)], axis=1
    ).astype(BF16)
    kg_ref[...] = dot(pair_backward_t(e_own, g_own, own_dphi[...]).astype(BF16), k_own)
    lane_c = lanes(CHUNK)
    pick_c = jnp.where((lane_c == 0) | (lane_c == HALF), 1.0, 0.0).astype(BF16)

    def back(ss, carry):
        @pl.when(any_visible(ss))
        def _():
            k, v = chunk_kv(ss)
            d = dot_nt(low[...], jnp.concatenate([v, pick_c], axis=1))
            kg_ref[...] += dot(
                pair_backward_t(kpn[ss, :HALF], kpn[ss, HALF:], d).astype(BF16), k
            )

        return carry

    lax.fori_loop(0, SIDE, back, 0)
    loss_ref[...] = loss_acc[...]

    def drain_f(j, carry):
        @pl.when(j < 4)
        def _():
            f_copy(slot_of(s, f - j), 0).wait_send()

        @pl.when(j < 3)
        def _():
            f_copy(slot_of(s, f + j), 1).wait_send()

        return carry

    lax.fori_loop(0, 4, drain_f, 0)

    def drain_s(t, carry):
        h, k = t // 8, t % 8
        ff = f + offset(k)

        @pl.when(t < 28)
        def _():
            s_copy(slot_of(s - h, ff), 0).wait_send()

        @pl.when((h < 3) | (k >= 4))
        def _():
            s_copy(slot_of(s + h, ff), 1).wait_send()

        return carry

    lax.fori_loop(0, 32, drain_s, 0)


ORDER = (4, 3, 5, 2, 6, 1, 7)
WIDE = 640


def reduce_kernel(
    qg_ref, kg_ref, loss_ref, qo_ref, ko_ref, lo_ref,
    parts, got1, mid, got2, full, got3, mine, got_loss,
    send1, recv1, send2, recv2, send3, recv3, send4, recv4,
):
    seq, head, f, s, stride_f, stride_s = place()

    def f_rank(j):
        return (((f + j) % SIDE) * stride_f + s * stride_s, head)

    def s_rank(j):
        return (f * stride_f + ((s + j) % SIDE) * stride_s, head)

    def h_rank(j):
        return (seq, (head + j) % SIDE)

    barrier = pltpu.get_barrier_semaphore()
    for rank in (f_rank, s_rank, h_rank):
        for j in range(1, SIDE):
            pl.semaphore_signal(barrier, inc=1, device_id=rank(j), device_id_type=MESH)

    loss = jnp.sum(loss_ref[...], keepdims=True).reshape(1, 1)
    loss_hi, loss_lo = hi_lo(loss)
    row = lax.broadcasted_iota(jnp.int32, (8, D), 0)
    extra = jnp.where(row == 0, loss_hi, jnp.where(row == 1, loss_lo, 0.0))
    for i in range(SIDE):
        parts[i, :, pl.ds(0, 512)] = qg_ref[pl.ds(16 * i, 16), :].astype(BF16)
        k = kg_ref[pl.ds(8 * i, 8), :]
        parts[i, :, pl.ds(512, D)] = jnp.concatenate([k, extra], axis=0).astype(BF16)
    pl.semaphore_wait(barrier, 3 * (SIDE - 1))

    def copies(src, dst, me, send, recv, rank):
        def make(j):
            return pltpu.make_async_remote_copy(
                src_ref=src(j), dst_ref=dst.at[me], send_sem=send.at[j], recv_sem=recv.at[me],
                device_id=rank(j), device_id_type=MESH,
            )

        def arrival(j):
            slot = (me + j) % SIDE
            return pltpu.make_async_remote_copy(
                src_ref=src(j), dst_ref=dst.at[slot], send_sem=send.at[j], recv_sem=recv.at[slot],
                device_id=rank(j), device_id_type=MESH,
            )

        return make, arrival

    make1, arrive1 = copies(lambda j: parts.at[(f + j) % SIDE], got1, f, send1, recv1, f_rank)
    for j in ORDER:
        make1(j).start()
    total = parts[f].astype(F32)
    for j in range(1, SIDE):
        arrive1(j).wait_recv()
        total = total + got1[(f + j) % SIDE].astype(F32)

    def value_of(total):
        tail = total[8:, 512:]
        return tail[0:1, 0:1] + tail[1:2, 0:1]

    def pack(total):
        hi, lo = hi_lo(value_of(total))
        extra = jnp.where(row == 0, hi, jnp.where(row == 1, lo, 0.0))
        tail = jnp.concatenate([total[:8, 512:], extra], axis=0)
        return jnp.concatenate([total[:, :512], tail], axis=1).astype(BF16)

    mid[...] = pack(total)
    make2, arrive2 = copies(lambda j: mid, got2, s, send2, recv2, s_rank)
    for j in ORDER:
        make2(j).start()
    total = mid[...].astype(F32)
    for j in range(1, SIDE):
        arrive2(j).wait_recv()
        total = total + got2[(s + j) % SIDE].astype(F32)

    full[...] = total.astype(BF16)
    make3, arrive3 = copies(lambda j: full, got3, f, send3, recv3, f_rank)
    for j in ORDER:
        make3(j).start()
    mine[...] = jnp.broadcast_to(value_of(total), (8, D))
    make4, arrive4 = copies(lambda j: mine, got_loss, head, send4, recv4, h_rank)
    for j in range(1, SIDE):
        make4(j).start()

    def put(i, block):
        qo_ref[pl.ds(pl.multiple_of(i * 16, 16), 16), :] = block[:, :512]
        ko_ref[pl.ds(pl.multiple_of(i * 8, 8), 8), :] = block[:8, 512:]

    put(f, total)
    for j in range(1, SIDE):
        arrive3(j).wait_recv()
        slot = (f + j) % SIDE
        put(slot, got3[slot].astype(F32))
    value = mine[...]
    for j in range(1, SIDE):
        arrive4(j).wait_recv()
        value = value + got_loss[(head + j) % SIDE]
    lo_ref[...] = value * (1.0 / TOKENS)
    for make in (make1, make2, make3, make4):
        for j in range(1, SIDE):
            make(j).wait_send()


def attend(queries, key_matrix, value_matrix, query_feature_weight, key_feature_weight):
    vmem = pl.BlockSpec(memory_space=pltpu.VMEM)
    anywhere = pl.BlockSpec(memory_space=pl.ANY)
    dma = pltpu.SemaphoreType.DMA
    return pl.pallas_call(
        main_kernel,
        out_shape=(
            jax.ShapeDtypeStruct((T, GROUP * D), BF16),
            jax.ShapeDtypeStruct((D, GROUP * HALF), F32),
            jax.ShapeDtypeStruct((HALF, D), F32),
            jax.ShapeDtypeStruct((8, D), F32),
        ),
        in_specs=[vmem, anywhere, anywhere, vmem, vmem],
        out_specs=(vmem, vmem, vmem, vmem),
        scratch_shapes=[
            pltpu.VMEM((BLOCKS, 2 * T, D), BF16),
            pltpu.VMEM((ROWS, D), BF16),
            pltpu.VMEM((ROWS, D), F32),
            pltpu.VMEM((SIDE, D, CHUNK), F32),
            pltpu.VMEM((ROWS, D), F32),
            pltpu.VMEM((ROWS, 2 * D), F32),
            pltpu.VMEM((2, PAIR, CHUNK), F32),
            pltpu.VMEM((2, PAIR, CHUNK), BF16),
            pltpu.VMEM((D, 2 * D), F32),
            pltpu.VMEM((D, 2 * D), F32),
            pltpu.VMEM((D, 2 * D), BF16),
            pltpu.VMEM((D, T), F32),
            pltpu.VMEM((HALF, D), BF16),
            pltpu.VMEM((8, D), F32),
            dma((2,)),
            dma((BLOCKS,)),
            dma((2, SIDE)),
            dma((2, BLOCKS)),
        ],
        compiler_params=pltpu.CompilerParams(
            collective_id=0, has_side_effects=True, vmem_limit_bytes=56 * 1024 * 1024
        ),
        name="attend",
    )(queries, key_matrix, value_matrix, query_feature_weight, key_feature_weight)


def combine(qg, kg, loss):
    vmem = pl.BlockSpec(memory_space=pltpu.VMEM)
    dma = pltpu.SemaphoreType.DMA
    return pl.pallas_call(
        reduce_kernel,
        out_shape=(
            jax.ShapeDtypeStruct((D, GROUP * HALF), F32),
            jax.ShapeDtypeStruct((HALF, D), F32),
            jax.ShapeDtypeStruct((8, D), F32),
        ),
        in_specs=[vmem] * 3,
        out_specs=(vmem,) * 3,
        scratch_shapes=[
            pltpu.VMEM((SIDE, 16, WIDE), BF16),
            pltpu.VMEM((SIDE, 16, WIDE), BF16),
            pltpu.VMEM((16, WIDE), BF16),
            pltpu.VMEM((SIDE, 16, WIDE), BF16),
            pltpu.VMEM((16, WIDE), BF16),
            pltpu.VMEM((SIDE, 16, WIDE), BF16),
            pltpu.VMEM((8, D), F32),
            pltpu.VMEM((SIDE, 8, D), F32),
        ]
        + [dma((SIDE,))] * 8,
        compiler_params=pltpu.CompilerParams(collective_id=1, has_side_effects=True),
        name="combine",
    )(qg, kg, loss)


def local(*operands):
    student, qg, kg, loss = attend(*operands)
    qo, ko, lo = combine(qg, kg, loss)
    return student, qo, ko.T, lo[0, 0]


def solution(mesh):
    placed = (
        P("seq", "head"),
        P("seq", "head"),
        P("seq", "head"),
        P(None, "head"),
        P(None, "head"),
    )
    return jax.shard_map(
        local,
        mesh=mesh,
        in_specs=placed,
        out_specs=(P("seq", "head"), P(None, "head"), P(None, "head"), P()),
        check_vma=False,
    )
```

```python
import functools

import jax
import jax.numpy as jnp
from jax import lax
from jax.experimental import pallas as pl
from jax.experimental.pallas import tpu as pltpu
from jax.sharding import PartitionSpec as P

D = 128
GROUP = 8
HALF = 64
T = 144
SIDE = 8
BLOCKS = SIDE * SIDE
TOKENS = BLOCKS * T
CHUNK = SIDE * T
ROWS = GROUP * T
PAIR = 2 * T
TILES = ROWS // PAIR
NEG = -1e30
SCALE2 = (D ** -0.5) * 1.4426950408889634
MESH = pl.DeviceIdType.MESH
F32 = jnp.float32
BF16 = jnp.bfloat16


def dot(a, b):
    return lax.dot_general(a, b, (((1,), (0,)), ((), ())), preferred_element_type=F32)


def dot_nt(a, b):
    return lax.dot_general(a, b, (((1,), (1,)), ((), ())), preferred_element_type=F32)


def dot_tn(a, b):
    return lax.dot_general(a, b, (((0,), (0,)), ((), ())), preferred_element_type=F32)


def lanes(rows):
    return lax.broadcasted_iota(jnp.int32, (rows, D), 1)


def halves(x, reduce, neutral):
    plus = lanes(x.shape[0]) < HALF
    a = reduce(jnp.where(plus, x, neutral), axis=1, keepdims=True)
    b = reduce(jnp.where(plus, neutral, x), axis=1, keepdims=True)
    return a, b, plus


def feature_pair(x):
    a, b, plus = halves(x, jnp.max, -jnp.inf)
    e = jnp.exp(x - jnp.where(plus, a, b))
    sa, sb, _ = halves(e, jnp.sum, 0.0)
    return e * jnp.where(plus, 1.0 / sa, 1.0 / sb)


def pair_backward(pn, d):
    a, b, plus = halves(pn * d, jnp.sum, 0.0)
    t = pn * (d - jnp.where(plus, a, b))
    return t - pltpu.roll(t, HALF, 1)


def feature_pair_t(x):
    a = jnp.max(x, axis=0, keepdims=True)
    b = jnp.min(x, axis=0, keepdims=True)
    e, g = jnp.exp(x - a), jnp.exp(b - x)
    e = e * (1.0 / jnp.sum(e, axis=0, keepdims=True))
    g = g * (1.0 / jnp.sum(g, axis=0, keepdims=True))
    return e, g


def pair_backward_t(e, g, d):
    dp, dn = d[:HALF], d[HALF:]
    a = jnp.sum(e * dp, axis=0, keepdims=True)
    b = jnp.sum(g * dn, axis=0, keepdims=True)
    return e * (dp - a) - g * (dn - b)


def hi_lo(x):
    hi = x.astype(BF16).astype(F32)
    return hi, x - hi


def place():
    seq = lax.axis_index("seq")
    head = lax.axis_index("head")
    core = head % 2
    y, z = seq % SIDE, seq // SIDE
    f = y + core * (z - y)
    s = z + core * (y - z)
    stride_f = 1 + (SIDE - 1) * core
    stride_s = SIDE - (SIDE - 1) * core
    return seq, head, f, s, stride_f, stride_s


def offset(k):
    return k // 2 - (k % 2) * k


FAR = (4, 3, 5, 2, 6, 1, 7)
NEAR = FAR[::-1]


def plan():
    waves = [[("own", 0, 0, 0)]]
    for w in range(1, 9):
        wave = []
        if w <= 4:
            wave.append(("f", 0, 0, 2 * w - 1))
        if w <= 3:
            wave.append(("f", 1, 0, 2 * w))
        for h in range(1, 5):
            d = w - h
            if not 0 <= d <= 4:
                continue
            for k in (2 * d - 1, 2 * d) if 1 <= d <= 3 else ((0,) if d == 0 else (7,)):
                if h <= 3 or k < 4:
                    wave.append(("s", 0, h, k))
                if h <= 3 or k >= 4:
                    wave.append(("s", 1, h, k))
        waves.append(wave)
    return waves


WAVES = plan()
SLOT = {}
SHIFT = []
for item in (item for wave in WAVES for item in wave):
    ring, way, hops, k = item
    SLOT[(0, 0, k) if hops == 0 else (way, hops, k)] = len(SHIFT)
    SHIFT.append((-hops if way == 0 else hops, offset(k)))
FLAT = [item for wave in WAVES for item in wave]
BEFORE = [FLAT[a:b] for a, b in ((5, 13), (13, 25), (25, 32), (32, 39), (39, 45), (45, 51), (51, 59), (59, 64))]


def sends_after(item):
    ring, way, hops, k = item
    out = []
    if hops == 0:
        mine = SLOT[(0, 0, k)]
        far = abs(offset(k))
        for step in (0, 1):
            if (ring == "own" or step == way) and far < (4 if step == 0 else 3):
                there = SLOT[(0, 0, 2 * (far + 1) - 1 if step == 0 else 2 * (far + 1))]
                out.append((mine, there, 0, step))
        for step in (0, 1):
            out.append((mine, SLOT[(step, 1, k)], 1, step))
    else:
        there = (way, hops + 1, k)
        if there in SLOT:
            out.append((SLOT[(way, hops, k)], SLOT[there], 1, way))
    return out


SENDS = [send for item in FLAT for send in sends_after(item)]


def main_kernel(
    q_ref, k_hbm, v_hbm, wq_ref, wk_ref,
    student_ref, qg_ref, kg_ref, loss_ref,
    kv, qs, qpn, kpn, run_max, acc, scores, probs, bias_all, prefix, later, low, own_dphi, loss_acc, kg_acc,
    parts, got1, mid, got2, full, got3, kparts, kgot1, kmid, kgot2, kfull, kgot3, mine, got_loss,
    local_sem, recv_sem, send_sem, out_sem, in_sem,
):
    seq, head, f, s, stride_f, stride_s = place()

    def rank(ff, ss):
        return (ff * stride_f + ss * stride_s, head)

    f_up, f_dn = rank((f + 1) % SIDE, s), rank((f + SIDE - 1) % SIDE, s)
    s_up, s_dn = rank(f, (s + 1) % SIDE), rank(f, (s + SIDE - 1) % SIDE)

    load_k = pltpu.make_async_copy(k_hbm, kv.at[0, pl.ds(0, T)], local_sem.at[0])
    load_v = pltpu.make_async_copy(v_hbm, kv.at[0, pl.ds(T, T)], local_sem.at[1])
    load_k.start()
    load_v.start()
    def f_rank(j):
        return rank((f + j) % SIDE, s)

    def s_rank(j):
        return rank(f, (s + j) % SIDE)

    def h_rank(j):
        return (seq, (head + j) % SIDE)

    barrier = pltpu.get_barrier_semaphore()
    for to in (f_rank, s_rank, h_rank):
        for j in range(1, SIDE):
            pl.semaphore_signal(barrier, inc=1, device_id=to(j), device_id_type=MESH)
    load_k.wait()
    load_v.wait()
    pl.semaphore_wait(barrier, 3 * (SIDE - 1))

    peers = ((f_up, f_dn), (s_up, s_dn))

    def copy(send):
        source, target, ring, way = send
        return pltpu.make_async_remote_copy(
            src_ref=kv.at[source], dst_ref=kv.at[target],
            send_sem=send_sem.at[SENDS.index(send)], recv_sem=recv_sem.at[target],
            device_id=peers[ring][way], device_id_type=MESH,
        )

    def forward(item):
        for send in sends_after(item):
            copy(send).start()

    def relay(items):
        for item in items:
            _, way, hops, k = item
            slot = SLOT[(0, 0, k) if hops == 0 else (way, hops, k)]
            pltpu.make_async_remote_copy(
                src_ref=kv.at[slot], dst_ref=kv.at[slot], send_sem=send_sem.at[0],
                recv_sem=recv_sem.at[slot], device_id=s_up, device_id_type=MESH,
            ).wait_recv()
            forward(item)

    forward(FLAT[0])

    block = lax.broadcasted_iota(jnp.int32, (1, CHUNK), 1) // T
    on = []
    for n in range(SIDE):
        row = jnp.zeros((1, CHUNK), F32)
        count = 0
        for j in range(SIDE):
            ds, df = SHIFT[n * SIDE + j]
            there = ((s + ds + SIDE) % SIDE) * stride_s + ((f + df + SIDE) % SIDE) * stride_f
            hidden = there >= seq
            row = jnp.where((block == j) & hidden, NEG, row)
            count = count + jnp.where(hidden, 0, 1)
        bias_all[n] = row
        on.append(count)

    def active(ci):
        return sum(jnp.where(ci == n, on[n], 0) for n in range(SIDE)) > 0

    k_own = kv[0, pl.ds(0, T), :]
    v_own = kv[0, pl.ds(T, T), :]
    e_own, g_own = feature_pair_t(dot_nt(wk_ref[...], k_own))
    kphi_own = jnp.concatenate([e_own, g_own], axis=0).astype(BF16)
    ones_t = jnp.ones((T, D), BF16)

    row_token = lax.broadcasted_iota(jnp.int32, (PAIR, T), 0)
    row_token = jnp.where(row_token >= T, row_token - T, row_token)
    causal = lax.broadcasted_iota(jnp.int32, (PAIR, T), 1) <= row_token

    prefix[...] = jnp.zeros_like(prefix)
    later[...] = jnp.zeros_like(later)
    own_dphi[...] = jnp.zeros_like(own_dphi)
    loss_acc[...] = jnp.zeros_like(loss_acc)

    def first(j, carry):
        @pl.when(j == 3)
        def _():
            relay(FLAT[1:5])

        rows = pl.ds(pl.multiple_of(j * PAIR, PAIR), PAIR)
        q_a = q_ref[:, pl.ds(pl.multiple_of(j * 2 * D, D), D)]
        q_b = q_ref[:, pl.ds(pl.multiple_of(j * 2 * D + D, D), D)]
        q = jnp.concatenate([q_a, q_b], axis=0)
        qs[rows, :] = q
        w = wq_ref[:, pl.ds(pl.multiple_of(j * D, D), D)]
        la, lb = dot(q_a, w), dot(q_b, w)
        plus = lanes(T) < HALF
        xa = jnp.where(plus, la, -pltpu.roll(la, HALF, 1))
        xb = jnp.where(plus, pltpu.roll(lb, HALF, 1), -lb)
        qpn[rows, :] = feature_pair(jnp.concatenate([xa, xb], axis=0))
        scores = jnp.where(causal, dot_nt(q, k_own) * SCALE2, NEG)
        top = jnp.max(scores, axis=1, keepdims=True)
        p = jnp.exp2(scores - top).astype(BF16)
        run_max[rows, :] = jnp.broadcast_to(top, (PAIR, D))
        acc[rows, :] = dot(p, jnp.concatenate([v_own, ones_t], axis=1))

        return carry

    lax.fori_loop(0, TILES, first, 0)

    def chunk_kv(ss):
        base = pl.multiple_of(ss * SIDE, SIDE)
        k = kv[pl.ds(base, SIDE), pl.ds(0, T), :].reshape(CHUNK, D)
        v = kv[pl.ds(base, SIDE), pl.ds(T, T), :].reshape(CHUNK, D)
        return k, v

    def step(ci, carry):
        for n in range(SIDE):
            pl.when(ci == n)(functools.partial(relay, BEFORE[n]))

        @pl.when(active(ci))
        def _():
            k, v = chunk_kv(ci)
            v1 = jnp.concatenate([v, jnp.ones((CHUNK, D), BF16)], axis=1)
            bias = bias_all[ci]
            seen = bias == 0.0
            cuts = [(i, min(256, CHUNK - i)) for i in range(0, CHUNK, 256)]

            def score(r):
                rows = pl.ds(r * PAIR, PAIR)
                q = qs[rows, :]
                top = None
                for i, n in cuts:
                    x = dot_nt(q, k[i:i + n]) * SCALE2 + bias[:, i:i + n]
                    scores[r % 2, :, pl.ds(i, n)] = x
                    for c in range(0, n, D):
                        top = x[:, c:c + D] if top is None else jnp.maximum(top, x[:, c:c + D])
                old = run_max[rows, :]
                new = jnp.maximum(old, jnp.max(top, axis=1, keepdims=True))
                run_max[rows, :] = new
                return new, jnp.exp2(old - new)

            def weigh(r, new, alpha):
                rows = pl.ds(r * PAIR, PAIR)
                for i in range(0, CHUNK, D):
                    x = scores[r % 2, :, pl.ds(i, D)]
                    probs[r % 2, :, pl.ds(i, D)] = jnp.exp2(x - new).astype(BF16)
                out = dot(probs[r % 2], v1)
                acc[rows, :] = acc[rows, :] * jnp.concatenate([alpha, alpha], axis=1) + out

            held = score(0)
            e, g = feature_pair_t(dot_nt(wk_ref[...], k))
            pn = jnp.where(seen, jnp.concatenate([e, g], axis=0), 0.0)
            kpn[ci] = pn
            prefix[...] += dot(pn.astype(BF16), v1)
            for r in range(TILES):
                ahead = score(r + 1) if r + 1 < TILES else None
                weigh(r, *held)
                held = ahead

        return carry

    lax.fori_loop(0, SIDE, step, 0)

    lane_d = lanes(D)
    norm_hi, norm_lo = hi_lo(prefix[:, D:])
    low[...] = jnp.concatenate(
        [prefix[:, :D], jnp.where(lane_d < HALF, norm_hi, norm_lo)], axis=1
    ).astype(BF16)
    lane = lanes(PAIR)
    lane_t = lanes(T)
    pick_t = jnp.where((lane_t == 0) | (lane_t == HALF), 1.0, 0.0).astype(BF16)
    v_pick = jnp.concatenate([v_own, pick_t], axis=1)

    def finish(j, carry):
        rows = pl.ds(pl.multiple_of(j * PAIR, PAIR), PAIR)
        pn = qpn[rows, :]
        phi = pn.astype(BF16)
        intra = jnp.where(causal, dot(phi, kphi_own), 0.0)
        far = dot(phi, low[...])
        numer = dot(intra.astype(BF16), v_own) + far[:, :D]
        far_d = far[:, D:]
        denom = jnp.sum(intra, axis=1, keepdims=True) + (far_d + pltpu.roll(far_d, HALF, 1))
        inv = 1.0 / denom
        student = numer * inv
        student_low = student.astype(BF16)
        student_ref[:, pl.ds(pl.multiple_of(j * 2 * D, D), D)] = student_low[:T]
        student_ref[:, pl.ds(pl.multiple_of(j * 2 * D + D, D), D)] = student_low[T:]
        a = acc[rows, :]
        teacher = (a[:, :D] / a[:, D:]).astype(BF16).astype(F32)
        differ = student - teacher
        loss_acc[...] += jnp.sum((differ * differ).reshape(PAIR // 8, 8, D), axis=0)
        grad = differ * (2.0 / TOKENS)
        numer_low = (grad * inv).astype(BF16)
        dg = -jnp.sum(grad * student, axis=1, keepdims=True) * inv
        dg_hi, dg_lo = hi_lo(dg)
        zero = jnp.zeros_like(dg)
        g_key = jnp.where(lane == 0, dg_hi, jnp.where(lane == HALF, dg_lo, zero)).astype(BF16)
        g_later = jnp.where(lane < HALF, dg_hi, dg_lo).astype(BF16)
        g_norm = jnp.where(
            (lane == 0) | (lane == HALF), dg_hi, jnp.where(lane == 1, dg_lo, zero)
        ).astype(BF16)
        coupling = dot_nt(jnp.concatenate([numer_low, g_key], axis=1), v_pick)
        coupling = jnp.where(causal, coupling, 0.0).astype(BF16)
        later[...] += dot_tn(phi, jnp.concatenate([numer_low, g_later], axis=1))
        own_dphi[...] += dot_tn(phi, coupling)
        dphi = dot_nt(coupling, kphi_own)
        dphi = dphi + dot_nt(jnp.concatenate([numer_low, g_norm], axis=1), low[...])
        dl = pair_backward(pn, dphi).astype(BF16)
        q = qs[rows, :]
        ga, gb = dot_tn(q[:T], dl[:T]), dot_tn(q[T:], dl[T:])
        both = jnp.where(lane_d < HALF, ga, -gb).astype(BF16).reshape(SIDE, 16, D)
        parts[:, :, pl.ds(pl.multiple_of(j * D, D), D)] = both
        return carry

    lax.fori_loop(0, TILES, finish, 0)

    def exchange(n, source, target, me, to):
        def make(j):
            return pltpu.make_async_remote_copy(
                src_ref=source(j), dst_ref=target.at[me], send_sem=out_sem.at[n, j],
                recv_sem=in_sem.at[n, me], device_id=to(j), device_id_type=MESH,
            )

        def gather(own):
            total = own
            for j in NEAR:
                slot = (me + j) % SIDE
                pltpu.make_async_remote_copy(
                    src_ref=source(j), dst_ref=target.at[slot], send_sem=out_sem.at[n, j],
                    recv_sem=in_sem.at[n, slot], device_id=to(j), device_id_type=MESH,
                ).wait_recv()
                if own is not None:
                    total = total + target[slot].astype(F32)
            return total

        for j in FAR:
            make(j).start()

        def finished():
            for j in NEAR:
                make(j).wait_send()

        return gather, finished

    q_one, q_one_end = exchange(0, lambda j: parts.at[(f + j) % SIDE], got1, f, f_rank)

    norm = later[:, D:]
    norm_hi, norm_lo = hi_lo(norm + pltpu.roll(norm, HALF, 1))
    low[...] = jnp.concatenate(
        [later[:, :D], jnp.where(lane_d < HALF, norm_hi, norm_lo)], axis=1
    ).astype(BF16)
    kg_acc[...] = dot(pair_backward_t(e_own, g_own, own_dphi[...]).astype(BF16), k_own)
    lane_c = lanes(CHUNK)
    pick_c = jnp.where((lane_c == 0) | (lane_c == HALF), 1.0, 0.0).astype(BF16)

    def back(ss, carry):
        @pl.when(active(ss))
        def _():
            k, v = chunk_kv(ss)
            d = dot_nt(low[...], jnp.concatenate([v, pick_c], axis=1))
            kg_acc[...] += dot(
                pair_backward_t(kpn[ss, :HALF], kpn[ss, HALF:], d).astype(BF16), k
            )

        return carry

    lax.fori_loop(0, SIDE, back, 0)
    row = lax.broadcasted_iota(jnp.int32, (8, D), 0)

    def extra(value):
        hi, lo = hi_lo(value)
        return jnp.where(row == 0, hi, jnp.where(row == 1, lo, 0.0))

    def value_of(total):
        return total[8:9, 0:1] + total[9:10, 0:1]

    tail = extra(jnp.sum(loss_acc[...], keepdims=True).reshape(1, 1))
    for i in range(SIDE):
        kparts[i] = jnp.concatenate([kg_acc[pl.ds(8 * i, 8), :], tail], axis=0).astype(BF16)
    k_one, k_one_end = exchange(1, lambda j: kparts.at[(f + j) % SIDE], kgot1, f, f_rank)
    mid[...] = q_one(parts[f].astype(F32)).astype(BF16)
    q_two, q_two_end = exchange(2, lambda j: mid, got2, s, s_rank)
    total = k_one(kparts[f].astype(F32))
    kmid[...] = jnp.concatenate([total[:8], extra(value_of(total))], axis=0).astype(BF16)
    k_two, k_two_end = exchange(3, lambda j: kmid, kgot2, s, s_rank)
    full[...] = q_two(mid[...].astype(F32)).astype(BF16)
    q_three, q_three_end = exchange(4, lambda j: full, got3, f, f_rank)
    total = k_two(kmid[...].astype(F32))
    kfull[...] = total.astype(BF16)
    k_three, k_three_end = exchange(5, lambda j: kfull, kgot3, f, f_rank)
    mine[...] = jnp.broadcast_to(value_of(total), (8, D))
    h_one, h_one_end = exchange(6, lambda j: mine, got_loss, head, h_rank)
    got3[f] = full[...]
    kgot3[f] = kfull[...]
    q_three(None)
    qg_ref[...] = got3[...]
    k_three(None)
    kg_ref[...] = kgot3[...]
    loss_ref[...] = h_one(mine[...])
    for end in (q_one_end, k_one_end, q_two_end, k_two_end, q_three_end, k_three_end, h_one_end):
        end()
    for send in SENDS:
        copy(send).wait_send()


def unpack_kernel(student_ref, qg_ref, kg_ref, loss_ref, so_ref, qo_ref, ko_ref, lo_ref):
    so_ref[...] = student_ref[...]
    qo_ref[...] = qg_ref[...].reshape(D, GROUP * HALF).astype(F32)
    for i in range(SIDE):
        ko_ref[pl.ds(8 * i, 8), :] = kg_ref[i].astype(F32)[:8]
    lo_ref[...] = loss_ref[0:1, 0:1] * (1.0 / TOKENS)


def attend(queries, key_matrix, value_matrix, query_feature_weight, key_feature_weight):
    vmem = pl.BlockSpec(memory_space=pltpu.VMEM)
    anywhere = pl.BlockSpec(memory_space=pl.ANY)
    dma = pltpu.SemaphoreType.DMA
    one, all_of = (16,), (SIDE, 16)
    exchanges = (all_of, all_of, one, all_of, one, all_of)
    return pl.pallas_call(
        main_kernel,
        out_shape=(
            jax.ShapeDtypeStruct((T, GROUP * D), BF16),
            jax.ShapeDtypeStruct((SIDE, 16, GROUP * HALF), BF16),
            jax.ShapeDtypeStruct((SIDE, 16, D), BF16),
            jax.ShapeDtypeStruct((8, D), F32),
        ),
        in_specs=[vmem, anywhere, anywhere, vmem, vmem],
        out_specs=(vmem, vmem, vmem, vmem),
        scratch_shapes=[
            pltpu.VMEM((BLOCKS, 2 * T, D), BF16),
            pltpu.VMEM((ROWS, D), BF16),
            pltpu.VMEM((ROWS, D), F32),
            pltpu.VMEM((SIDE, D, CHUNK), F32),
            pltpu.VMEM((ROWS, D), F32),
            pltpu.VMEM((ROWS, 2 * D), F32),
            pltpu.VMEM((2, PAIR, CHUNK), F32),
            pltpu.VMEM((2, PAIR, CHUNK), BF16),
            pltpu.VMEM((SIDE, 1, CHUNK), F32),
            pltpu.VMEM((D, 2 * D), F32),
            pltpu.VMEM((D, 2 * D), F32),
            pltpu.VMEM((D, 2 * D), BF16),
            pltpu.VMEM((D, T), F32),
            pltpu.VMEM((8, D), F32),
            pltpu.VMEM((HALF, D), F32),
        ]
        + [pltpu.VMEM(shape + (512,), BF16) for shape in exchanges]
        + [pltpu.VMEM(shape + (D,), BF16) for shape in exchanges]
        + [
            pltpu.VMEM((8, D), F32),
            pltpu.VMEM((SIDE, 8, D), F32),
            dma((2,)),
            dma((BLOCKS,)),
            dma((len(SENDS),)),
            dma((7, SIDE)),
            dma((7, SIDE)),
        ],
        compiler_params=pltpu.CompilerParams(
            collective_id=0, has_side_effects=True, vmem_limit_bytes=56 * 1024 * 1024
        ),
        name="attend",
    )(queries, key_matrix, value_matrix, query_feature_weight, key_feature_weight.T)


def unpack(*operands):
    vmem = pl.BlockSpec(memory_space=pltpu.VMEM)
    return pl.pallas_call(
        unpack_kernel,
        out_shape=(
            jax.ShapeDtypeStruct((T, GROUP * D), BF16),
            jax.ShapeDtypeStruct((D, GROUP * HALF), F32),
            jax.ShapeDtypeStruct((HALF, D), F32),
            jax.ShapeDtypeStruct((1, 1), F32),
        ),
        in_specs=[vmem] * 4,
        out_specs=(vmem,) * 4,
        name="unpack",
    )(*operands)


def local(*operands):
    student, qo, ko, lo = unpack(*attend(*operands))
    return student, qo, ko.T, lo.reshape(())


def solution(mesh):
    placed = (
        P("seq", "head"),
        P("seq", "head"),
        P("seq", "head"),
        P(None, "head"),
        P(None, "head"),
    )
    return jax.shard_map(
        local,
        mesh=mesh,
        in_specs=placed,
        out_specs=(P("seq", "head"), P(None, "head"), P(None, "head"), P()),
        check_vma=False,
    )
```

```python
import functools

import jax
import jax.numpy as jnp
from jax import lax
from jax.experimental import pallas as pl
from jax.experimental.pallas import tpu as pltpu
from jax.sharding import PartitionSpec as P

D = 128
GROUP = 8
HALF = 64
T = 144
SIDE = 8
BLOCKS = SIDE * SIDE
TOKENS = BLOCKS * T
CHUNK = SIDE * T
ROWS = GROUP * T
PAIR = 2 * T
TILES = ROWS // PAIR
NEG = -1e30
SCALE2 = (D ** -0.5) * 1.4426950408889634
MESH = pl.DeviceIdType.MESH
F32 = jnp.float32
BF16 = jnp.bfloat16


def dot(a, b):
    return lax.dot_general(a, b, (((1,), (0,)), ((), ())), preferred_element_type=F32)


def dot_nt(a, b):
    return lax.dot_general(a, b, (((1,), (1,)), ((), ())), preferred_element_type=F32)


def dot_tn(a, b):
    return lax.dot_general(a, b, (((0,), (0,)), ((), ())), preferred_element_type=F32)


def lanes(rows):
    return lax.broadcasted_iota(jnp.int32, (rows, D), 1)


def halves(x, reduce, neutral):
    plus = lanes(x.shape[0]) < HALF
    a = reduce(jnp.where(plus, x, neutral), axis=1, keepdims=True)
    b = reduce(jnp.where(plus, neutral, x), axis=1, keepdims=True)
    return a, b, plus


def feature_pair(x):
    a, b, plus = halves(x, jnp.max, -jnp.inf)
    e = jnp.exp(x - jnp.where(plus, a, b))
    sa, sb, _ = halves(e, jnp.sum, 0.0)
    return e * jnp.where(plus, 1.0 / sa, 1.0 / sb)


def pair_backward(pn, d):
    a, b, plus = halves(pn * d, jnp.sum, 0.0)
    t = pn * (d - jnp.where(plus, a, b))
    return t - pltpu.roll(t, HALF, 1)


def feature_pair_t(x):
    a = jnp.max(x, axis=0, keepdims=True)
    b = jnp.min(x, axis=0, keepdims=True)
    e, g = jnp.exp(x - a), jnp.exp(b - x)
    e = e * (1.0 / jnp.sum(e, axis=0, keepdims=True))
    g = g * (1.0 / jnp.sum(g, axis=0, keepdims=True))
    return e, g


def pair_backward_t(e, g, d):
    dp, dn = d[:HALF], d[HALF:]
    a = jnp.sum(e * dp, axis=0, keepdims=True)
    b = jnp.sum(g * dn, axis=0, keepdims=True)
    return e * (dp - a) - g * (dn - b)


def hi_lo(x):
    hi = x.astype(BF16).astype(F32)
    return hi, x - hi


def place():
    seq = lax.axis_index("seq")
    head = lax.axis_index("head")
    core = head % 2
    y, z = seq % SIDE, seq // SIDE
    f = y + core * (z - y)
    s = z + core * (y - z)
    stride_f = 1 + (SIDE - 1) * core
    stride_s = SIDE - (SIDE - 1) * core
    return seq, head, f, s, stride_f, stride_s


def offset(k):
    return k // 2 - (k % 2) * k


FAR = (4, 3, 5, 2, 6, 1, 7)
NEAR = FAR[::-1]


ARRIVAL = (
    0, 10, 1, 110, 2, 20, 3, 111, 4, 11, 120, 12, 112, 30, 5, 113,
    6, 13, 121, 14, 114, 130, 21, 122, 7, 22, 115, 40, 123, 15, 116, 16,
    131, 23, 124, 24, 132, 31, 117, 17, 125, 32, 133, 25, 126, 26, 134, 33,
    127, 34, 135, 41, 136, 27, 144, 42, 137, 35, 145, 36, 146, 43, 147, 37,
)


def unpacked(code):
    way, hops, k = code // 100, code // 10 % 10, code % 10
    if hops:
        return ("s", way, hops, k)
    return ("own", 0, 0, 0) if k == 0 else ("f", 1 - k % 2, 0, k)


FLAT = [unpacked(code) for code in ARRIVAL]
SLOT = {}
SHIFT = []
for ring, way, hops, k in FLAT:
    SLOT[(0, 0, k) if hops == 0 else (way, hops, k)] = len(SHIFT)
    SHIFT.append((-hops if way == 0 else hops, offset(k)) if hops else (0, offset(k)))
CUTS = (9, 13, 25, 32, 39, 45, 51, 59, 64)
BEFORE = [FLAT[a:b] for a, b in zip(CUTS, CUTS[1:])]


def sends_after(item):
    ring, way, hops, k = item
    out = []
    if hops == 0:
        mine = SLOT[(0, 0, k)]
        far = abs(offset(k))
        for step in (0, 1):
            if (ring == "own" or step == way) and far < (4 if step == 0 else 3):
                there = SLOT[(0, 0, 2 * (far + 1) - 1 if step == 0 else 2 * (far + 1))]
                out.append((mine, there, 0, step))
        for step in (0, 1):
            out.append((mine, SLOT[(step, 1, k)], 1, step))
    else:
        there = (way, hops + 1, k)
        if there in SLOT:
            out.append((SLOT[(way, hops, k)], SLOT[there], 1, way))
    return out


SENDS = [send for item in FLAT for send in sends_after(item)]


def main_kernel(
    q_hbm, k_hbm, v_hbm, wq_hbm, wk_hbm,
    student_hbm, qg_ref, kg_ref, loss_ref,
    kv, qs, qpn, kpn, run_max, acc, scores, probs, bias_all, prefix, later, low, own_dphi, loss_acc, kg_acc,
    parts, got1, mid, got2, full, got3, kparts, kgot1, kmid, kgot2, kfull, kgot3, mine, got_loss,
    phi_t, q_t, near_n, near_d, q_ref, wq_ref, wk_ref, student_ref,
    local_sem, recv_sem, send_sem, out_sem, in_sem,
):
    seq, head, f, s, stride_f, stride_s = place()

    def rank(ff, ss):
        return (ff * stride_f + ss * stride_s, head)

    f_up, f_dn = rank((f + 1) % SIDE, s), rank((f + SIDE - 1) % SIDE, s)
    s_up, s_dn = rank(f, (s + 1) % SIDE), rank(f, (s + SIDE - 1) % SIDE)

    load_k = pltpu.make_async_copy(k_hbm, kv.at[0, pl.ds(0, T)], local_sem.at[0])
    load_v = pltpu.make_async_copy(v_hbm, kv.at[0, pl.ds(T, T)], local_sem.at[1])
    load_k.start()
    load_v.start()
    rest = [
        pltpu.make_async_copy(source, target, local_sem.at[n])
        for n, source, target in ((2, wk_hbm, wk_ref), (3, q_hbm, q_ref), (4, wq_hbm, wq_ref))
    ]
    for load in rest:
        load.start()
    def f_rank(j):
        return rank((f + j) % SIDE, s)

    def s_rank(j):
        return rank(f, (s + j) % SIDE)

    def h_rank(j):
        return (seq, (head + j) % SIDE)

    barrier = pltpu.get_barrier_semaphore()
    for to in (f_rank, s_rank, h_rank):
        for j in range(1, SIDE):
            pl.semaphore_signal(barrier, inc=1, device_id=to(j), device_id_type=MESH)
    load_k.wait()
    load_v.wait()
    pl.semaphore_wait(barrier, 3 * (SIDE - 1))

    peers = ((f_up, f_dn), (s_up, s_dn))

    def copy(send):
        source, target, ring, way = send
        return pltpu.make_async_remote_copy(
            src_ref=kv.at[source], dst_ref=kv.at[target],
            send_sem=send_sem.at[SENDS.index(send)], recv_sem=recv_sem.at[target],
            device_id=peers[ring][way], device_id_type=MESH,
        )

    def forward(item):
        for send in sends_after(item):
            copy(send).start()

    def relay(items):
        for item in items:
            _, way, hops, k = item
            slot = SLOT[(0, 0, k) if hops == 0 else (way, hops, k)]
            pltpu.make_async_remote_copy(
                src_ref=kv.at[slot], dst_ref=kv.at[slot], send_sem=send_sem.at[0],
                recv_sem=recv_sem.at[slot], device_id=s_up, device_id_type=MESH,
            ).wait_recv()
            forward(item)

    forward(FLAT[0])

    block = lax.broadcasted_iota(jnp.int32, (1, CHUNK), 1) // T
    on = []
    for n in range(SIDE):
        row = jnp.zeros((1, CHUNK), F32)
        count = 0
        for j in range(SIDE):
            ds, df = SHIFT[n * SIDE + j]
            there = ((s + ds + SIDE) % SIDE) * stride_s + ((f + df + SIDE) % SIDE) * stride_f
            hidden = there >= seq
            row = jnp.where((block == j) & hidden, NEG, row)
            count = count + jnp.where(hidden, 0, 1)
        bias_all[n] = row
        on.append(count)

    for load in rest:
        load.wait()

    def active(ci):
        return sum(jnp.where(ci == n, on[n], 0) for n in range(SIDE)) > 0

    k_own = kv[0, pl.ds(0, T), :]
    v_own = kv[0, pl.ds(T, T), :]
    e_own, g_own = feature_pair_t(dot_nt(wk_ref[...], k_own))
    kphi_own = jnp.concatenate([e_own, g_own], axis=0).astype(BF16)
    ones_t = jnp.ones((T, D), BF16)

    row_token = lax.broadcasted_iota(jnp.int32, (PAIR, T), 0)
    row_token = jnp.where(row_token >= T, row_token - T, row_token)
    causal = lax.broadcasted_iota(jnp.int32, (PAIR, T), 1) <= row_token

    prefix[...] = jnp.zeros_like(prefix)
    later[...] = jnp.zeros_like(later)
    own_dphi[...] = jnp.zeros_like(own_dphi)
    loss_acc[...] = jnp.zeros_like(loss_acc)

    def first(j, carry):
        pl.when(j == 2)(functools.partial(relay, FLAT[1:5]))
        pl.when(j == 3)(functools.partial(relay, FLAT[5:9]))
        rows = pl.ds(pl.multiple_of(j * PAIR, PAIR), PAIR)
        q_a = q_ref[:, pl.ds(pl.multiple_of(j * 2 * D, D), D)]
        q_b = q_ref[:, pl.ds(pl.multiple_of(j * 2 * D + D, D), D)]
        q = jnp.concatenate([q_a, q_b], axis=0)
        qs[rows, :] = q
        w = wq_ref[:, pl.ds(pl.multiple_of(j * D, D), D)]
        la, lb = dot(q_a, w), dot(q_b, w)
        plus = lanes(T) < HALF
        xa = jnp.where(plus, la, -pltpu.roll(la, HALF, 1))
        xb = jnp.where(plus, pltpu.roll(lb, HALF, 1), -lb)
        pn = feature_pair(jnp.concatenate([xa, xb], axis=0))
        qpn[rows, :] = pn
        phi = pn.astype(BF16)
        phi_t[j] = phi.T
        q_t[2 * j] = q_a.T
        q_t[2 * j + 1] = q_b.T
        intra = jnp.where(causal, dot(phi, kphi_own), 0.0)
        near_n[rows, :] = dot(intra.astype(BF16), v_own)
        near_d[rows, :] = jnp.broadcast_to(jnp.sum(intra, axis=1, keepdims=True), (PAIR, D))
        scores = jnp.where(causal, dot_nt(q, k_own) * SCALE2, NEG)
        top = jnp.max(scores, axis=1, keepdims=True)
        p = jnp.exp2(scores - top).astype(BF16)
        run_max[rows, :] = jnp.broadcast_to(top, (PAIR, D))
        acc[rows, :] = dot(p, jnp.concatenate([v_own, ones_t], axis=1))

        return carry

    lax.fori_loop(0, TILES, first, 0)

    def chunk_kv(ss):
        base = pl.multiple_of(ss * SIDE, SIDE)
        k = kv[pl.ds(base, SIDE), pl.ds(0, T), :].reshape(CHUNK, D)
        v = kv[pl.ds(base, SIDE), pl.ds(T, T), :].reshape(CHUNK, D)
        return k, v

    def step(ci, carry):
        for n in range(SIDE):
            pl.when(ci == n)(functools.partial(relay, BEFORE[n]))

        live = active(ci)

        @pl.when(jnp.logical_not(live))
        def _():
            kpn[ci] = jnp.zeros((D, CHUNK), F32)

        @pl.when(live)
        def _():
            k, v = chunk_kv(ci)
            v1 = jnp.concatenate([v, jnp.ones((CHUNK, D), BF16)], axis=1)
            bias = bias_all[ci]
            seen = bias == 0.0
            cuts = [(i, min(256, CHUNK - i)) for i in range(0, CHUNK, 256)]

            def score(r):
                rows = pl.ds(r * PAIR, PAIR)
                q = qs[rows, :]
                top = None
                for i, n in cuts:
                    x = dot_nt(q, k[i:i + n]) * SCALE2 + bias[:, i:i + n]
                    scores[r % 2, :, pl.ds(i, n)] = x
                    for c in range(0, n, D):
                        top = x[:, c:c + D] if top is None else jnp.maximum(top, x[:, c:c + D])
                old = run_max[rows, :]
                new = jnp.maximum(old, jnp.max(top, axis=1, keepdims=True))
                run_max[rows, :] = new
                return new, jnp.exp2(old - new)

            def weigh(r, new, alpha):
                rows = pl.ds(r * PAIR, PAIR)
                for i in range(0, CHUNK, D):
                    x = scores[r % 2, :, pl.ds(i, D)]
                    probs[r % 2, :, pl.ds(i, D)] = jnp.exp2(x - new).astype(BF16)
                out = dot(probs[r % 2], v1)
                acc[rows, :] = acc[rows, :] * jnp.concatenate([alpha, alpha], axis=1) + out

            held = score(0)
            e, g = feature_pair_t(dot_nt(wk_ref[...], k))
            pn = jnp.where(seen, jnp.concatenate([e, g], axis=0), 0.0)
            kpn[ci] = pn
            prefix[...] += dot(pn.astype(BF16), v1)
            for r in range(TILES):
                ahead = score(r + 1) if r + 1 < TILES else None
                weigh(r, *held)
                held = ahead

        return carry

    lax.fori_loop(0, SIDE, step, 0)

    lane_d = lanes(D)
    norm_hi, norm_lo = hi_lo(prefix[:, D:])
    low[...] = jnp.concatenate(
        [prefix[:, :D], jnp.where(lane_d < HALF, norm_hi, norm_lo)], axis=1
    ).astype(BF16)
    lane = lanes(PAIR)
    lane_t = lanes(T)
    pick_t = jnp.where((lane_t == 0) | (lane_t == HALF), 1.0, 0.0).astype(BF16)
    v_pick = jnp.concatenate([v_own, pick_t], axis=1)

    def exchange(n, source, target, me, to):
        def make(j):
            return pltpu.make_async_remote_copy(
                src_ref=source(j), dst_ref=target.at[me], send_sem=out_sem.at[n, j],
                recv_sem=in_sem.at[n, me], device_id=to(j), device_id_type=MESH,
            )

        def gather(own):
            total = own
            for j in NEAR:
                slot = (me + j) % SIDE
                pltpu.make_async_remote_copy(
                    src_ref=source(j), dst_ref=target.at[slot], send_sem=out_sem.at[n, j],
                    recv_sem=in_sem.at[n, slot], device_id=to(j), device_id_type=MESH,
                ).wait_recv()
                if own is not None:
                    total = total + target[slot].astype(F32)
            return total

        def begin():
            for j in FAR:
                make(j).start()

        def finished():
            for j in NEAR:
                make(j).wait_send()

        return begin, gather, finished

    def tile_exchange(r):
        return exchange(r, lambda j: parts.at[r, (f + j) % SIDE], got1.at[r], f, f_rank)

    tiles = [tile_exchange(r) for r in range(TILES)]

    def finish(j):
        if j:
            tiles[j - 1][0]()
        rows = pl.ds(pl.multiple_of(j * PAIR, PAIR), PAIR)
        pn = qpn[rows, :]
        phi = pn.astype(BF16)
        far = dot(phi, low[...])
        numer = near_n[rows, :] + far[:, :D]
        far_d = far[:, D:]
        denom = near_d[rows, :] + (far_d + pltpu.roll(far_d, HALF, 1))
        inv = 1.0 / denom
        student = numer * inv
        student_low = student.astype(BF16)
        student_ref[:, pl.ds(pl.multiple_of(j * 2 * D, D), D)] = student_low[:T]
        student_ref[:, pl.ds(pl.multiple_of(j * 2 * D + D, D), D)] = student_low[T:]
        a = acc[rows, :]
        teacher = (a[:, :D] / a[:, D:]).astype(BF16).astype(F32)
        differ = student - teacher
        loss_acc[...] += jnp.sum((differ * differ).reshape(PAIR // 8, 8, D), axis=0)
        grad = differ * (2.0 / TOKENS)
        numer_low = (grad * inv).astype(BF16)
        dg = -jnp.sum(grad * student, axis=1, keepdims=True) * inv
        dg_hi, dg_lo = hi_lo(dg)
        zero = jnp.zeros_like(dg)
        g_key = jnp.where(lane == 0, dg_hi, jnp.where(lane == HALF, dg_lo, zero)).astype(BF16)
        g_later = jnp.where(lane < HALF, dg_hi, dg_lo).astype(BF16)
        g_norm = jnp.where(
            (lane == 0) | (lane == HALF), dg_hi, jnp.where(lane == 1, dg_lo, zero)
        ).astype(BF16)
        coupling = dot_nt(jnp.concatenate([numer_low, g_key], axis=1), v_pick)
        coupling = jnp.where(causal, coupling, 0.0).astype(BF16)
        later[...] += dot(phi_t[j], jnp.concatenate([numer_low, g_later], axis=1))
        own_dphi[...] += dot(phi_t[j], coupling)
        dphi = dot_nt(coupling, kphi_own)
        dphi = dphi + dot_nt(jnp.concatenate([numer_low, g_norm], axis=1), low[...])
        dl = pair_backward(pn, dphi).astype(BF16)
        ga, gb = dot(q_t[2 * j], dl[:T]), dot(q_t[2 * j + 1], dl[T:])
        both = jnp.where(lane_d < HALF, ga, -gb).astype(BF16).reshape(SIDE, 16, D)
        parts[j] = both

    for j in range(TILES):
        finish(j)
    put = pltpu.make_async_copy(student_ref, student_hbm, local_sem.at[5])

    norm = later[:, D:]
    norm_hi, norm_lo = hi_lo(norm + pltpu.roll(norm, HALF, 1))
    low[...] = jnp.concatenate(
        [later[:, :D], jnp.where(lane_d < HALF, norm_hi, norm_lo)], axis=1
    ).astype(BF16)
    tiles[TILES - 1][0]()
    put.start()
    kg_acc[...] = dot(pair_backward_t(e_own, g_own, own_dphi[...]).astype(BF16), k_own)
    lane_c = lanes(CHUNK)
    pick_c = jnp.where((lane_c == 0) | (lane_c == HALF), 1.0, 0.0).astype(BF16)

    def back(ss, carry):
        k, v = chunk_kv(ss)
        d = dot_nt(low[...], jnp.concatenate([v, pick_c], axis=1))
        kg_acc[...] += dot(pair_backward_t(kpn[ss, :HALF], kpn[ss, HALF:], d).astype(BF16), k)
        return carry

    lax.fori_loop(0, SIDE, back, 0, unroll=True)
    row = lax.broadcasted_iota(jnp.int32, (8, D), 0)

    def extra(value):
        hi, lo = hi_lo(value)
        return jnp.where(row == 0, hi, jnp.where(row == 1, lo, 0.0))

    def value_of(total):
        return total[8:9, 0:1] + total[9:10, 0:1]

    tail = extra(jnp.sum(loss_acc[...], keepdims=True).reshape(1, 1))
    for i in range(SIDE):
        kparts[i] = jnp.concatenate([kg_acc[pl.ds(8 * i, 8), :], tail], axis=0).astype(BF16)
    k_begin, k_one, k_one_end = exchange(
        4, lambda j: kparts.at[(f + j) % SIDE], kgot1, f, f_rank
    )
    k_begin()
    for send in SENDS:
        copy(send).wait_send()
    for r in range(TILES):
        mid[:, pl.ds(r * D, D)] = tiles[r][1](parts[r, f].astype(F32)).astype(BF16)
    begin, q_two, q_two_end = exchange(5, lambda j: mid, got2, s, s_rank)
    begin()
    total = k_one(kparts[f].astype(F32))
    kmid[...] = jnp.concatenate([total[:8], extra(value_of(total))], axis=0).astype(BF16)
    begin, k_two, k_two_end = exchange(6, lambda j: kmid, kgot2, s, s_rank)
    begin()
    for tile in tiles:
        tile[2]()
    k_one_end()
    put.wait()
    full[...] = q_two(mid[...].astype(F32)).astype(BF16)
    begin, q_three, q_three_end = exchange(7, lambda j: full, got3, f, f_rank)
    begin()
    total = k_two(kmid[...].astype(F32))
    kfull[...] = total.astype(BF16)
    begin, k_three, k_three_end = exchange(8, lambda j: kfull, kgot3, f, f_rank)
    begin()
    mine[...] = jnp.broadcast_to(value_of(total), (8, D))
    begin, h_one, h_one_end = exchange(9, lambda j: mine, got_loss, head, h_rank)
    begin()
    got3[f] = full[...]
    kgot3[f] = kfull[...]
    q_two_end()
    k_two_end()
    q_three(None)
    qg_ref[...] = got3[...]
    k_three(None)
    kg_ref[...] = kgot3[...]
    loss_ref[...] = h_one(mine[...])
    for end in (q_three_end, k_three_end, h_one_end):
        end()


def unpack_kernel(student_ref, qg_ref, kg_ref, loss_ref, so_ref, qo_ref, ko_ref, lo_ref):
    so_ref[...] = student_ref[...]
    qo_ref[...] = qg_ref[...].reshape(D, GROUP * HALF).astype(F32)
    for i in range(SIDE):
        ko_ref[pl.ds(8 * i, 8), :] = kg_ref[i].astype(F32)[:8]
    lo_ref[...] = loss_ref[0:1, 0:1] * (1.0 / TOKENS)


def attend(queries, key_matrix, value_matrix, query_feature_weight, key_feature_weight):
    vmem = pl.BlockSpec(memory_space=pltpu.VMEM)
    anywhere = pl.BlockSpec(memory_space=pl.ANY)
    dma = pltpu.SemaphoreType.DMA
    one, all_of = (16,), (SIDE, 16)
    exchanges = (all_of, all_of, one, all_of, one, all_of)
    return pl.pallas_call(
        main_kernel,
        out_shape=(
            jax.ShapeDtypeStruct((T, GROUP * D), BF16),
            jax.ShapeDtypeStruct((SIDE, 16, GROUP * HALF), BF16),
            jax.ShapeDtypeStruct((SIDE, 16, D), BF16),
            jax.ShapeDtypeStruct((8, D), F32),
        ),
        in_specs=[anywhere] * 5,
        out_specs=(anywhere, vmem, vmem, vmem),
        scratch_shapes=[
            pltpu.VMEM((BLOCKS, 2 * T, D), BF16),
            pltpu.VMEM((ROWS, D), BF16),
            pltpu.VMEM((ROWS, D), F32),
            pltpu.VMEM((SIDE, D, CHUNK), F32),
            pltpu.VMEM((ROWS, D), F32),
            pltpu.VMEM((ROWS, 2 * D), F32),
            pltpu.VMEM((2, PAIR, CHUNK), F32),
            pltpu.VMEM((2, PAIR, CHUNK), BF16),
            pltpu.VMEM((SIDE, 1, CHUNK), F32),
            pltpu.VMEM((D, 2 * D), F32),
            pltpu.VMEM((D, 2 * D), F32),
            pltpu.VMEM((D, 2 * D), BF16),
            pltpu.VMEM((D, T), F32),
            pltpu.VMEM((8, D), F32),
            pltpu.VMEM((HALF, D), F32),
        ]
        + [pltpu.VMEM((TILES,) + all_of + (D,), BF16)] * 2
        + [pltpu.VMEM(shape + (512,), BF16) for shape in exchanges[2:]]
        + [pltpu.VMEM(shape + (D,), BF16) for shape in exchanges]
        + [
            pltpu.VMEM((8, D), F32),
            pltpu.VMEM((SIDE, 8, D), F32),
            pltpu.VMEM((TILES, D, PAIR), BF16),
            pltpu.VMEM((GROUP, D, T), BF16),
            pltpu.VMEM((ROWS, D), F32),
            pltpu.VMEM((ROWS, D), F32),
            pltpu.VMEM((T, GROUP * D), BF16),
            pltpu.VMEM((D, GROUP * HALF), BF16),
            pltpu.VMEM((HALF, D), BF16),
            pltpu.VMEM((T, GROUP * D), BF16),
            dma((6,)),
            dma((BLOCKS,)),
            dma((len(SENDS),)),
            dma((10, SIDE)),
            dma((10, SIDE)),
        ],
        compiler_params=pltpu.CompilerParams(
            collective_id=0, has_side_effects=True, vmem_limit_bytes=56 * 1024 * 1024
        ),
        name="attend",
    )(queries, key_matrix, value_matrix, query_feature_weight, key_feature_weight.T)


def unpack(*operands):
    vmem = pl.BlockSpec(memory_space=pltpu.VMEM)
    return pl.pallas_call(
        unpack_kernel,
        out_shape=(
            jax.ShapeDtypeStruct((T, GROUP * D), BF16),
            jax.ShapeDtypeStruct((D, GROUP * HALF), F32),
            jax.ShapeDtypeStruct((HALF, D), F32),
            jax.ShapeDtypeStruct((1, 1), F32),
        ),
        in_specs=[vmem] * 4,
        out_specs=(vmem,) * 4,
        name="unpack",
    )(*operands)


def local(*operands):
    student, qo, ko, lo = unpack(*attend(*operands))
    return student, qo, ko.T, lo.reshape(())


def solution(mesh):
    placed = (
        P("seq", "head"),
        P("seq", "head"),
        P("seq", "head"),
        P(None, "head"),
        P(None, "head"),
    )
    return jax.shard_map(
        local,
        mesh=mesh,
        in_specs=placed,
        out_specs=(P("seq", "head"), P(None, "head"), P(None, "head"), P()),
        check_vma=False,
    )
```

```python
import functools

import jax
import jax.numpy as jnp
from jax import lax
from jax.experimental import pallas as pl
from jax.experimental.pallas import tpu as pltpu
from jax.sharding import PartitionSpec as P

D = 128
GROUP = 8
HALF = 64
T = 144
SIDE = 8
BLOCKS = SIDE * SIDE
TOKENS = BLOCKS * T
CHUNK = SIDE * T
ROWS = GROUP * T
PAIR = 2 * T
TILES = ROWS // PAIR
NEG = -1e30
SCALE2 = (D ** -0.5) * 1.4426950408889634
MESH = pl.DeviceIdType.MESH
F32 = jnp.float32
BF16 = jnp.bfloat16


def dot(a, b):
    return lax.dot_general(a, b, (((1,), (0,)), ((), ())), preferred_element_type=F32)


def dot_nt(a, b):
    return lax.dot_general(a, b, (((1,), (1,)), ((), ())), preferred_element_type=F32)


def dot_tn(a, b):
    return lax.dot_general(a, b, (((0,), (0,)), ((), ())), preferred_element_type=F32)


def lanes(rows):
    return lax.broadcasted_iota(jnp.int32, (rows, D), 1)


def halves(x, reduce, neutral):
    plus = lanes(x.shape[0]) < HALF
    a = reduce(jnp.where(plus, x, neutral), axis=1, keepdims=True)
    b = reduce(jnp.where(plus, neutral, x), axis=1, keepdims=True)
    return a, b, plus


def feature_pair(x):
    a, b, plus = halves(x, jnp.max, -jnp.inf)
    e = jnp.exp(x - jnp.where(plus, a, b))
    sa, sb, _ = halves(e, jnp.sum, 0.0)
    return e * jnp.where(plus, 1.0 / sa, 1.0 / sb)


def pair_backward(pn, d):
    a, b, plus = halves(pn * d, jnp.sum, 0.0)
    t = pn * (d - jnp.where(plus, a, b))
    return t - pltpu.roll(t, HALF, 1)


def feature_pair_t(x):
    a = jnp.max(x, axis=0, keepdims=True)
    b = jnp.min(x, axis=0, keepdims=True)
    e, g = jnp.exp(x - a), jnp.exp(b - x)
    e = e * (1.0 / jnp.sum(e, axis=0, keepdims=True))
    g = g * (1.0 / jnp.sum(g, axis=0, keepdims=True))
    return e, g


def pair_backward_t(e, g, d):
    dp, dn = d[:HALF], d[HALF:]
    a = jnp.sum(e * dp, axis=0, keepdims=True)
    b = jnp.sum(g * dn, axis=0, keepdims=True)
    return e * (dp - a) - g * (dn - b)


def hi_lo(x):
    hi = x.astype(BF16).astype(F32)
    return hi, x - hi


def place():
    seq = lax.axis_index("seq")
    head = lax.axis_index("head")
    core = head % 2
    y, z = seq % SIDE, seq // SIDE
    f = y + core * (z - y)
    s = z + core * (y - z)
    stride_f = 1 + (SIDE - 1) * core
    stride_s = SIDE - (SIDE - 1) * core
    return seq, head, f, s, stride_f, stride_s


def offset(k):
    return k // 2 - (k % 2) * k


FAR = (4, 3, 5, 2, 6, 1, 7)
NEAR = FAR[::-1]


ARRIVAL = (
    0, 10, 1, 110, 2, 20, 3, 111, 4, 11, 120, 12, 112, 30, 5, 113,
    6, 13, 121, 14, 114, 130, 21, 122, 7, 22, 115, 40, 123, 15, 116, 16,
    131, 23, 124, 24, 132, 31, 117, 17, 125, 32, 133, 25, 126, 26, 134, 33,
    127, 34, 135, 41, 136, 27, 144, 42, 137, 35, 145, 36, 146, 43, 147, 37,
)


def unpacked(code):
    way, hops, k = code // 100, code // 10 % 10, code % 10
    if hops:
        return ("s", way, hops, k)
    return ("own", 0, 0, 0) if k == 0 else ("f", 1 - k % 2, 0, k)


FLAT = [unpacked(code) for code in ARRIVAL]
SLOT = {}
SHIFT = []
for ring, way, hops, k in FLAT:
    SLOT[(0, 0, k) if hops == 0 else (way, hops, k)] = len(SHIFT)
    SHIFT.append((-hops if way == 0 else hops, offset(k)) if hops else (0, offset(k)))
CUTS = (9, 13, 25, 32, 39, 45, 51, 59, 64)
BEFORE = [FLAT[a:b] for a, b in zip(CUTS, CUTS[1:])]


def sends_after(item):
    ring, way, hops, k = item
    out = []
    if hops == 0:
        mine = SLOT[(0, 0, k)]
        far = abs(offset(k))
        for step in (0, 1):
            if (ring == "own" or step == way) and far < (4 if step == 0 else 3):
                there = SLOT[(0, 0, 2 * (far + 1) - 1 if step == 0 else 2 * (far + 1))]
                out.append((mine, there, 0, step))
        for step in (0, 1):
            out.append((mine, SLOT[(step, 1, k)], 1, step))
    else:
        there = (way, hops + 1, k)
        if there in SLOT:
            out.append((SLOT[(way, hops, k)], SLOT[there], 1, way))
    return out


SENDS = [send for item in FLAT for send in sends_after(item)]


def main_kernel(
    q_hbm, k_hbm, v_hbm, wq_hbm, wk_hbm,
    student_hbm, qg_ref, kg_ref, loss_ref,
    kv, qs, qpn, kpn, run_max, acc, scores, probs, bias_all, prefix, later, low, own_dphi, loss_acc, kg_acc,
    parts, got1, mid, got2, full, got3, kparts, kgot1, kmid, kgot2, kfull, kgot3, mine, got_loss,
    phi_t, q_t, near_n, near_d, q_ref, wq_ref, wk_ref, student_ref,
    local_sem, recv_sem, send_sem, out_sem, in_sem,
):
    seq, head, f, s, stride_f, stride_s = place()

    def rank(ff, ss):
        return (ff * stride_f + ss * stride_s, head)

    f_up, f_dn = rank((f + 1) % SIDE, s), rank((f + SIDE - 1) % SIDE, s)
    s_up, s_dn = rank(f, (s + 1) % SIDE), rank(f, (s + SIDE - 1) % SIDE)

    load_k = pltpu.make_async_copy(k_hbm, kv.at[0, pl.ds(0, T)], local_sem.at[0])
    load_v = pltpu.make_async_copy(v_hbm, kv.at[0, pl.ds(T, T)], local_sem.at[1])
    load_k.start()
    load_v.start()
    rest = [
        pltpu.make_async_copy(source, target, local_sem.at[n])
        for n, source, target in ((2, wk_hbm, wk_ref), (3, q_hbm, q_ref), (4, wq_hbm, wq_ref))
    ]
    for load in rest:
        load.start()
    def f_rank(j):
        return rank((f + j) % SIDE, s)

    def s_rank(j):
        return rank(f, (s + j) % SIDE)

    def h_rank(j):
        return (seq, (head + j) % SIDE)

    barrier = pltpu.get_barrier_semaphore()
    for to in (f_rank, s_rank, h_rank):
        for j in range(1, SIDE):
            pl.semaphore_signal(barrier, inc=1, device_id=to(j), device_id_type=MESH)
    load_k.wait()
    load_v.wait()
    pl.semaphore_wait(barrier, 3 * (SIDE - 1))

    peers = ((f_up, f_dn), (s_up, s_dn))

    def copy(send):
        source, target, ring, way = send
        return pltpu.make_async_remote_copy(
            src_ref=kv.at[source], dst_ref=kv.at[target],
            send_sem=send_sem.at[SENDS.index(send)], recv_sem=recv_sem.at[target],
            device_id=peers[ring][way], device_id_type=MESH,
        )

    def forward(item):
        for send in sends_after(item):
            copy(send).start()

    def relay(items):
        for item in items:
            _, way, hops, k = item
            slot = SLOT[(0, 0, k) if hops == 0 else (way, hops, k)]
            pltpu.make_async_remote_copy(
                src_ref=kv.at[slot], dst_ref=kv.at[slot], send_sem=send_sem.at[0],
                recv_sem=recv_sem.at[slot], device_id=s_up, device_id_type=MESH,
            ).wait_recv()
            forward(item)

    forward(FLAT[0])

    block = lax.broadcasted_iota(jnp.int32, (1, CHUNK), 1) // T
    on = []
    for n in range(SIDE):
        row = jnp.zeros((1, CHUNK), F32)
        count = 0
        for j in range(SIDE):
            ds, df = SHIFT[n * SIDE + j]
            there = ((s + ds + SIDE) % SIDE) * stride_s + ((f + df + SIDE) % SIDE) * stride_f
            hidden = there >= seq
            row = jnp.where((block == j) & hidden, NEG, row)
            count = count + jnp.where(hidden, 0, 1)
        bias_all[n] = row
        on.append(count)

    for load in rest:
        load.wait()

    def active(ci):
        return sum(jnp.where(ci == n, on[n], 0) for n in range(SIDE)) > 0

    k_own = kv[0, pl.ds(0, T), :]
    v_own = kv[0, pl.ds(T, T), :]
    e_own, g_own = feature_pair_t(dot_nt(wk_ref[...], k_own))
    kphi_own = jnp.concatenate([e_own, g_own], axis=0).astype(BF16)
    ones_t = jnp.ones((T, D), BF16)

    row_token = lax.broadcasted_iota(jnp.int32, (PAIR, T), 0)
    row_token = jnp.where(row_token >= T, row_token - T, row_token)
    causal = lax.broadcasted_iota(jnp.int32, (PAIR, T), 1) <= row_token

    prefix[...] = jnp.zeros_like(prefix)
    later[...] = jnp.zeros_like(later)
    own_dphi[...] = jnp.zeros_like(own_dphi)
    loss_acc[...] = jnp.zeros_like(loss_acc)

    def first(j, carry):
        pl.when(j == 2)(functools.partial(relay, FLAT[1:5]))
        pl.when(j == 3)(functools.partial(relay, FLAT[5:9]))
        rows = pl.ds(pl.multiple_of(j * PAIR, PAIR), PAIR)
        q_a = q_ref[:, pl.ds(pl.multiple_of(j * 2 * D, D), D)]
        q_b = q_ref[:, pl.ds(pl.multiple_of(j * 2 * D + D, D), D)]
        q = jnp.concatenate([q_a, q_b], axis=0)
        qs[rows, :] = q
        w = wq_ref[:, pl.ds(pl.multiple_of(j * D, D), D)]
        la, lb = dot(q_a, w), dot(q_b, w)
        plus = lanes(T) < HALF
        xa = jnp.where(plus, la, -pltpu.roll(la, HALF, 1))
        xb = jnp.where(plus, pltpu.roll(lb, HALF, 1), -lb)
        pn = feature_pair(jnp.concatenate([xa, xb], axis=0))
        qpn[rows, :] = pn
        phi = pn.astype(BF16)
        phi_t[j] = phi.T
        q_t[2 * j] = q_a.T
        q_t[2 * j + 1] = q_b.T
        intra = jnp.where(causal, dot(phi, kphi_own), 0.0)
        near_n[rows, :] = dot(intra.astype(BF16), v_own)
        near_d[rows, :] = jnp.broadcast_to(jnp.sum(intra, axis=1, keepdims=True), (PAIR, D))
        scores = jnp.where(causal, dot_nt(q, k_own) * SCALE2, NEG)
        top = jnp.max(scores, axis=1, keepdims=True)
        p = jnp.exp2(scores - top).astype(BF16)
        run_max[rows, :] = jnp.broadcast_to(top, (PAIR, D))
        acc[rows, :] = dot(p, jnp.concatenate([v_own, ones_t], axis=1))

        return carry

    lax.fori_loop(0, TILES, first, 0)

    def chunk_kv(ss):
        base = pl.multiple_of(ss * SIDE, SIDE)
        k = kv[pl.ds(base, SIDE), pl.ds(0, T), :].reshape(CHUNK, D)
        v = kv[pl.ds(base, SIDE), pl.ds(T, T), :].reshape(CHUNK, D)
        return k, v

    def work(ci, ready=None, finish=None):
        k, v = chunk_kv(ci)
        v1 = jnp.concatenate([v, jnp.ones((CHUNK, D), BF16)], axis=1)
        bias = bias_all[ci]
        seen = bias == 0.0
        cuts = [(i, min(256, CHUNK - i)) for i in range(0, CHUNK, 256)]

        def score(r):
            rows = pl.ds(r * PAIR, PAIR)
            q = qs[rows, :]
            top = None
            for i, n in cuts:
                x = dot_nt(q, k[i:i + n]) * SCALE2 + bias[:, i:i + n]
                scores[r % 2, :, pl.ds(i, n)] = x
                for c in range(0, n, D):
                    top = x[:, c:c + D] if top is None else jnp.maximum(top, x[:, c:c + D])
            old = run_max[rows, :]
            new = jnp.maximum(old, jnp.max(top, axis=1, keepdims=True))
            run_max[rows, :] = new
            return new, jnp.exp2(old - new)

        def weigh(r, new, alpha):
            rows = pl.ds(r * PAIR, PAIR)
            for i in range(0, CHUNK, D):
                x = scores[r % 2, :, pl.ds(i, D)]
                probs[r % 2, :, pl.ds(i, D)] = jnp.exp2(x - new).astype(BF16)
            out = dot(probs[r % 2], v1)
            acc[rows, :] = acc[rows, :] * jnp.concatenate([alpha, alpha], axis=1) + out

        held = score(0)
        e, g = feature_pair_t(dot_nt(wk_ref[...], k))
        pn = jnp.where(seen, jnp.concatenate([e, g], axis=0), 0.0)
        kpn[ci] = pn
        prefix[...] += dot(pn.astype(BF16), v1)
        if ready is not None:
            ready()
        for r in range(TILES):
            ahead = score(r + 1) if r + 1 < TILES else None
            weigh(r, *held)
            if finish is not None:
                finish(r)
            held = ahead

    def step(ci, carry):
        for n in range(SIDE - 1):
            pl.when(ci == n)(functools.partial(relay, BEFORE[n]))

        live = active(ci)

        @pl.when(jnp.logical_not(live))
        def _():
            kpn[ci] = jnp.zeros((D, CHUNK), F32)

        pl.when(live)(functools.partial(work, ci))
        return carry

    lax.fori_loop(0, SIDE - 1, step, 0)

    lane_d = lanes(D)
    def ready():
        norm_hi, norm_lo = hi_lo(prefix[:, D:])
        low[...] = jnp.concatenate(
            [prefix[:, :D], jnp.where(lane_d < HALF, norm_hi, norm_lo)], axis=1
        ).astype(BF16)

    lane = lanes(PAIR)
    lane_t = lanes(T)
    pick_t = jnp.where((lane_t == 0) | (lane_t == HALF), 1.0, 0.0).astype(BF16)
    v_pick = jnp.concatenate([v_own, pick_t], axis=1)

    def exchange(n, source, target, me, to):
        def make(j):
            return pltpu.make_async_remote_copy(
                src_ref=source(j), dst_ref=target.at[me], send_sem=out_sem.at[n, j],
                recv_sem=in_sem.at[n, me], device_id=to(j), device_id_type=MESH,
            )

        def gather(own):
            total = own
            for j in NEAR:
                slot = (me + j) % SIDE
                pltpu.make_async_remote_copy(
                    src_ref=source(j), dst_ref=target.at[slot], send_sem=out_sem.at[n, j],
                    recv_sem=in_sem.at[n, slot], device_id=to(j), device_id_type=MESH,
                ).wait_recv()
                if own is not None:
                    total = total + target[slot].astype(F32)
            return total

        def begin():
            for j in FAR:
                make(j).start()

        def finished():
            for j in NEAR:
                make(j).wait_send()

        return begin, gather, finished

    def tile_one(r):
        return exchange(r, lambda j: parts.at[r, (f + j) % SIDE], got1.at[r], f, f_rank)

    def tile_two(r):
        return exchange(TILES + r, lambda j: mid.at[r], got2.at[r], s, s_rank)

    def tile_three(r):
        return exchange(2 * TILES + r, lambda j: full.at[r], got3.at[r], f, f_rank)

    tiles = [tile_one(r) for r in range(TILES)]
    twos = [tile_two(r) for r in range(TILES)]
    threes = [tile_three(r) for r in range(TILES)]

    def finish(j):
        if j:
            tiles[j - 1][0]()
        rows = pl.ds(pl.multiple_of(j * PAIR, PAIR), PAIR)
        pn = qpn[rows, :]
        phi = pn.astype(BF16)
        far = dot(phi, low[...])
        numer = near_n[rows, :] + far[:, :D]
        far_d = far[:, D:]
        denom = near_d[rows, :] + (far_d + pltpu.roll(far_d, HALF, 1))
        inv = 1.0 / denom
        student = numer * inv
        student_low = student.astype(BF16)
        student_ref[:, pl.ds(pl.multiple_of(j * 2 * D, D), D)] = student_low[:T]
        student_ref[:, pl.ds(pl.multiple_of(j * 2 * D + D, D), D)] = student_low[T:]
        a = acc[rows, :]
        teacher = (a[:, :D] / a[:, D:]).astype(BF16).astype(F32)
        differ = student - teacher
        loss_acc[...] += jnp.sum((differ * differ).reshape(PAIR // 8, 8, D), axis=0)
        grad = differ * (2.0 / TOKENS)
        numer_low = (grad * inv).astype(BF16)
        dg = -jnp.sum(grad * student, axis=1, keepdims=True) * inv
        dg_hi, dg_lo = hi_lo(dg)
        zero = jnp.zeros_like(dg)
        g_key = jnp.where(lane == 0, dg_hi, jnp.where(lane == HALF, dg_lo, zero)).astype(BF16)
        g_later = jnp.where(lane < HALF, dg_hi, dg_lo).astype(BF16)
        g_norm = jnp.where(
            (lane == 0) | (lane == HALF), dg_hi, jnp.where(lane == 1, dg_lo, zero)
        ).astype(BF16)
        coupling = dot_nt(jnp.concatenate([numer_low, g_key], axis=1), v_pick)
        coupling = jnp.where(causal, coupling, 0.0).astype(BF16)
        later[...] += dot(phi_t[j], jnp.concatenate([numer_low, g_later], axis=1))
        own_dphi[...] += dot(phi_t[j], coupling)
        dphi = dot_nt(coupling, kphi_own)
        dphi = dphi + dot_nt(jnp.concatenate([numer_low, g_norm], axis=1), low[...])
        dl = pair_backward(pn, dphi).astype(BF16)
        ga, gb = dot(q_t[2 * j], dl[:T]), dot(q_t[2 * j + 1], dl[T:])
        both = jnp.where(lane_d < HALF, ga, -gb).astype(BF16).reshape(SIDE, 16, D)
        parts[j] = both

    relay(BEFORE[SIDE - 1])
    work(SIDE - 1, ready, finish)
    put = pltpu.make_async_copy(student_ref, student_hbm, local_sem.at[5])

    norm = later[:, D:]
    norm_hi, norm_lo = hi_lo(norm + pltpu.roll(norm, HALF, 1))
    low[...] = jnp.concatenate(
        [later[:, :D], jnp.where(lane_d < HALF, norm_hi, norm_lo)], axis=1
    ).astype(BF16)
    tiles[TILES - 1][0]()
    put.start()
    kg_acc[...] = dot(pair_backward_t(e_own, g_own, own_dphi[...]).astype(BF16), k_own)
    lane_c = lanes(CHUNK)
    pick_c = jnp.where((lane_c == 0) | (lane_c == HALF), 1.0, 0.0).astype(BF16)

    def back(ss, carry):
        k, v = chunk_kv(ss)
        d = dot_nt(low[...], jnp.concatenate([v, pick_c], axis=1))
        kg_acc[...] += dot(pair_backward_t(kpn[ss, :HALF], kpn[ss, HALF:], d).astype(BF16), k)
        return carry

    lax.fori_loop(0, SIDE, back, 0, unroll=True)
    row = lax.broadcasted_iota(jnp.int32, (8, D), 0)

    def extra(value):
        hi, lo = hi_lo(value)
        return jnp.where(row == 0, hi, jnp.where(row == 1, lo, 0.0))

    def value_of(total):
        return total[8:9, 0:1] + total[9:10, 0:1]

    tail = extra(jnp.sum(loss_acc[...], keepdims=True).reshape(1, 1))
    for i in range(SIDE):
        kparts[i] = jnp.concatenate([kg_acc[pl.ds(8 * i, 8), :], tail], axis=0).astype(BF16)
    k_begin, k_one, k_one_end = exchange(
        12, lambda j: kparts.at[(f + j) % SIDE], kgot1, f, f_rank
    )
    k_begin()
    for r in range(TILES):
        mid[r] = tiles[r][1](parts[r, f].astype(F32)).astype(BF16)
        twos[r][0]()
    total = k_one(kparts[f].astype(F32))
    kmid[...] = jnp.concatenate([total[:8], extra(value_of(total))], axis=0).astype(BF16)
    begin, k_two, k_two_end = exchange(13, lambda j: kmid, kgot2, s, s_rank)
    begin()
    for send in SENDS:
        copy(send).wait_send()
    for r in range(TILES):
        full[r] = twos[r][1](mid[r].astype(F32)).astype(BF16)
        threes[r][0]()
    total = k_two(kmid[...].astype(F32))
    kfull[...] = total.astype(BF16)
    begin, k_three, k_three_end = exchange(14, lambda j: kfull, kgot3, f, f_rank)
    begin()
    mine[...] = jnp.broadcast_to(value_of(total), (8, D))
    begin, h_one, h_one_end = exchange(15, lambda j: mine, got_loss, head, h_rank)
    begin()
    put.wait()
    for r in range(TILES):
        got3[r, f] = full[r]
        tiles[r][2]()
        twos[r][2]()
    kgot3[f] = kfull[...]
    k_one_end()
    k_two_end()
    for r in range(TILES):
        threes[r][1](None)
        qg_ref[r] = got3[r]
    k_three(None)
    kg_ref[...] = kgot3[...]
    loss_ref[...] = h_one(mine[...])
    for r in range(TILES):
        threes[r][2]()
    k_three_end()
    h_one_end()


def unpack_kernel(student_ref, qg_ref, kg_ref, loss_ref, so_ref, qo_ref, ko_ref, lo_ref):
    so_ref[...] = student_ref[...]
    for r in range(TILES):
        qo_ref[:, pl.ds(r * D, D)] = qg_ref[r].reshape(D, D).astype(F32)
    for i in range(SIDE):
        ko_ref[pl.ds(8 * i, 8), :] = kg_ref[i].astype(F32)[:8]
    lo_ref[...] = loss_ref[0:1, 0:1] * (1.0 / TOKENS)


def attend(queries, key_matrix, value_matrix, query_feature_weight, key_feature_weight):
    vmem = pl.BlockSpec(memory_space=pltpu.VMEM)
    anywhere = pl.BlockSpec(memory_space=pl.ANY)
    dma = pltpu.SemaphoreType.DMA
    one, all_of = (16,), (SIDE, 16)
    exchanges = (all_of, all_of, one, all_of, one, all_of)
    return pl.pallas_call(
        main_kernel,
        out_shape=(
            jax.ShapeDtypeStruct((T, GROUP * D), BF16),
            jax.ShapeDtypeStruct((TILES, SIDE, 16, D), BF16),
            jax.ShapeDtypeStruct((SIDE, 16, D), BF16),
            jax.ShapeDtypeStruct((8, D), F32),
        ),
        in_specs=[anywhere] * 5,
        out_specs=(anywhere, vmem, vmem, vmem),
        scratch_shapes=[
            pltpu.VMEM((BLOCKS, 2 * T, D), BF16),
            pltpu.VMEM((ROWS, D), BF16),
            pltpu.VMEM((ROWS, D), F32),
            pltpu.VMEM((SIDE, D, CHUNK), F32),
            pltpu.VMEM((ROWS, D), F32),
            pltpu.VMEM((ROWS, 2 * D), F32),
            pltpu.VMEM((2, PAIR, CHUNK), F32),
            pltpu.VMEM((2, PAIR, CHUNK), BF16),
            pltpu.VMEM((SIDE, 1, CHUNK), F32),
            pltpu.VMEM((D, 2 * D), F32),
            pltpu.VMEM((D, 2 * D), F32),
            pltpu.VMEM((D, 2 * D), BF16),
            pltpu.VMEM((D, T), F32),
            pltpu.VMEM((8, D), F32),
            pltpu.VMEM((HALF, D), F32),
        ]
        + [pltpu.VMEM((TILES,) + shape + (D,), BF16) for shape in exchanges]
        + [pltpu.VMEM(shape + (D,), BF16) for shape in exchanges]
        + [
            pltpu.VMEM((8, D), F32),
            pltpu.VMEM((SIDE, 8, D), F32),
            pltpu.VMEM((TILES, D, PAIR), BF16),
            pltpu.VMEM((GROUP, D, T), BF16),
            pltpu.VMEM((ROWS, D), F32),
            pltpu.VMEM((ROWS, D), F32),
            pltpu.VMEM((T, GROUP * D), BF16),
            pltpu.VMEM((D, GROUP * HALF), BF16),
            pltpu.VMEM((HALF, D), BF16),
            pltpu.VMEM((T, GROUP * D), BF16),
            dma((6,)),
            dma((BLOCKS,)),
            dma((len(SENDS),)),
            dma((16, SIDE)),
            dma((16, SIDE)),
        ],
        compiler_params=pltpu.CompilerParams(
            collective_id=0, has_side_effects=True, vmem_limit_bytes=56 * 1024 * 1024
        ),
        name="attend",
    )(queries, key_matrix, value_matrix, query_feature_weight, key_feature_weight.T)


def unpack(*operands):
    vmem = pl.BlockSpec(memory_space=pltpu.VMEM)
    return pl.pallas_call(
        unpack_kernel,
        out_shape=(
            jax.ShapeDtypeStruct((T, GROUP * D), BF16),
            jax.ShapeDtypeStruct((D, GROUP * HALF), F32),
            jax.ShapeDtypeStruct((HALF, D), F32),
            jax.ShapeDtypeStruct((1, 1), F32),
        ),
        in_specs=[vmem] * 4,
        out_specs=(vmem,) * 4,
        name="unpack",
    )(*operands)


def local(*operands):
    student, qo, ko, lo = unpack(*attend(*operands))
    return student, qo, ko.T, lo.reshape(())


def solution(mesh):
    placed = (
        P("seq", "head"),
        P("seq", "head"),
        P("seq", "head"),
        P(None, "head"),
        P(None, "head"),
    )
    return jax.shard_map(
        local,
        mesh=mesh,
        in_specs=placed,
        out_specs=(P("seq", "head"), P(None, "head"), P(None, "head"), P()),
        check_vma=False,
    )
```

```python
import functools

import jax
import jax.numpy as jnp
from jax import lax
from jax.experimental import pallas as pl
from jax.experimental.pallas import tpu as pltpu
from jax.sharding import PartitionSpec as P

D = 128
GROUP = 8
HALF = 64
T = 144
SIDE = 8
BLOCKS = SIDE * SIDE
TOKENS = BLOCKS * T
SEVEN = 7
CHUNKS = 9
CHUNK = SEVEN * T
ROWS = GROUP * T
PAIR = 2 * T
TILES = ROWS // PAIR
NEG = -1e30
SCALE2 = (D ** -0.5) * 1.4426950408889634
MESH = pl.DeviceIdType.MESH
F32 = jnp.float32
BF16 = jnp.bfloat16


def dot(a, b):
    return lax.dot_general(a, b, (((1,), (0,)), ((), ())), preferred_element_type=F32)


def dot_nt(a, b):
    return lax.dot_general(a, b, (((1,), (1,)), ((), ())), preferred_element_type=F32)


def dot_tn(a, b):
    return lax.dot_general(a, b, (((0,), (0,)), ((), ())), preferred_element_type=F32)


def lanes(rows):
    return lax.broadcasted_iota(jnp.int32, (rows, D), 1)


def halves(x, reduce, neutral):
    plus = lanes(x.shape[0]) < HALF
    a = reduce(jnp.where(plus, x, neutral), axis=1, keepdims=True)
    b = reduce(jnp.where(plus, neutral, x), axis=1, keepdims=True)
    return a, b, plus


def feature_pair(x):
    a, b, plus = halves(x, jnp.max, -jnp.inf)
    e = jnp.exp(x - jnp.where(plus, a, b))
    sa, sb, _ = halves(e, jnp.sum, 0.0)
    return e * jnp.where(plus, 1.0 / sa, 1.0 / sb)


def pair_backward(pn, d):
    a, b, plus = halves(pn * d, jnp.sum, 0.0)
    t = pn * (d - jnp.where(plus, a, b))
    return t - pltpu.roll(t, HALF, 1)


def feature_pair_t(x):
    a = jnp.max(x, axis=0, keepdims=True)
    b = jnp.min(x, axis=0, keepdims=True)
    e, g = jnp.exp(x - a), jnp.exp(b - x)
    e = e * (1.0 / jnp.sum(e, axis=0, keepdims=True))
    g = g * (1.0 / jnp.sum(g, axis=0, keepdims=True))
    return e, g


def pair_backward_t(e, g, d):
    dp, dn = d[:HALF], d[HALF:]
    a = jnp.sum(e * dp, axis=0, keepdims=True)
    b = jnp.sum(g * dn, axis=0, keepdims=True)
    return e * (dp - a) - g * (dn - b)


def hi_lo(x):
    hi = x.astype(BF16).astype(F32)
    return hi, x - hi


def place():
    seq = lax.axis_index("seq")
    head = lax.axis_index("head")
    core = head % 2
    y, z = seq % SIDE, seq // SIDE
    f = y + core * (z - y)
    s = z + core * (y - z)
    stride_f = 1 + (SIDE - 1) * core
    stride_s = SIDE - (SIDE - 1) * core
    return seq, head, f, s, stride_f, stride_s


def offset(k):
    return k // 2 - (k % 2) * k


FAR = (4, 3, 5, 2, 6, 1, 7)
NEAR = FAR[::-1]


ARRIVAL = (
    0, 10, 1, 110, 2, 20, 3, 111, 4, 11, 120, 12, 112, 30, 5, 113,
    6, 13, 121, 14, 114, 130, 21, 122, 7, 22, 115, 40, 123, 15, 116, 16,
    131, 23, 124, 24, 132, 31, 117, 17, 125, 32, 133, 25, 126, 26, 134, 33,
    127, 34, 135, 41, 136, 27, 144, 42, 137, 35, 145, 36, 146, 43, 147, 37,
)


def unpacked(code):
    way, hops, k = code // 100, code // 10 % 10, code % 10
    if hops:
        return ("s", way, hops, k)
    return ("own", 0, 0, 0) if k == 0 else ("f", 1 - k % 2, 0, k)


FLAT = [unpacked(code) for code in ARRIVAL]
SLOT = {}
SHIFT = []
for ring, way, hops, k in FLAT:
    SLOT[(0, 0, k) if hops == 0 else (way, hops, k)] = len(SHIFT)
    SHIFT.append((-hops if way == 0 else hops, offset(k)) if hops else (0, offset(k)))
CUTS = (9, 12, 21, 29, 35, 41, 47, 53, 59, 64)
BEFORE = [FLAT[a:b] for a, b in zip(CUTS, CUTS[1:])]


def sends_after(item):
    ring, way, hops, k = item
    out = []
    if hops == 0:
        mine = SLOT[(0, 0, k)]
        far = abs(offset(k))
        for step in (0, 1):
            if (ring == "own" or step == way) and far < (4 if step == 0 else 3):
                there = SLOT[(0, 0, 2 * (far + 1) - 1 if step == 0 else 2 * (far + 1))]
                out.append((mine, there, 0, step))
        for step in (0, 1):
            out.append((mine, SLOT[(step, 1, k)], 1, step))
    else:
        there = (way, hops + 1, k)
        if there in SLOT:
            out.append((SLOT[(way, hops, k)], SLOT[there], 1, way))
    return out


SENDS = [send for item in FLAT for send in sends_after(item)]


def main_kernel(
    q_hbm, k_hbm, v_hbm, wq_hbm, wk_hbm,
    student_hbm, qg_ref, kg_ref, loss_ref,
    kv, qs, qpn, kpn, run_max, acc, scores, probs, bias_all, prefix, later, low, own_dphi, loss_acc, kg_acc,
    parts, got1, mid, got2, full, got3, kparts, kgot1, kmid, kgot2, kfull, kgot3, mine, got_loss,
    phi_t, q_t, near_n, near_d, q_ref, wq_ref, wk_ref, student_ref,
    local_sem, recv_sem, send_sem, out_sem, in_sem,
):
    seq, head, f, s, stride_f, stride_s = place()

    def rank(ff, ss):
        return (ff * stride_f + ss * stride_s, head)

    f_up, f_dn = rank((f + 1) % SIDE, s), rank((f + SIDE - 1) % SIDE, s)
    s_up, s_dn = rank(f, (s + 1) % SIDE), rank(f, (s + SIDE - 1) % SIDE)

    load_k = pltpu.make_async_copy(k_hbm, kv.at[0, pl.ds(0, T)], local_sem.at[0])
    load_v = pltpu.make_async_copy(v_hbm, kv.at[0, pl.ds(T, T)], local_sem.at[1])
    load_k.start()
    load_v.start()
    rest = [
        pltpu.make_async_copy(source, target, local_sem.at[n])
        for n, source, target in ((2, wk_hbm, wk_ref), (3, q_hbm, q_ref), (4, wq_hbm, wq_ref))
    ]
    for load in rest:
        load.start()
    def f_rank(j):
        return rank((f + j) % SIDE, s)

    def s_rank(j):
        return rank(f, (s + j) % SIDE)

    def h_rank(j):
        return (seq, (head + j) % SIDE)

    barrier = pltpu.get_barrier_semaphore()
    f_ring = [(None, f)] + [(f_rank(j), (f + j) % SIDE) for j in range(1, SIDE)]
    s_ring = [(None, s)] + [(s_rank(j), (s + j) % SIDE) for j in range(1, SIDE)]
    h_ring = [(None, head)] + [(h_rank(j), (head + j) % SIDE) for j in range(1, SIDE)]
    for ring in (f_ring, s_ring, h_ring):
        for peer, _ in ring[1:]:
            pl.semaphore_signal(barrier, inc=1, device_id=peer, device_id_type=MESH)
    load_k.wait()
    load_v.wait()
    pl.semaphore_wait(barrier, 3 * (SIDE - 1))

    peers = ((f_up, f_dn), (s_up, s_dn))

    def copy(send):
        source, target, ring, way = send
        return pltpu.make_async_remote_copy(
            src_ref=kv.at[source], dst_ref=kv.at[target],
            send_sem=send_sem.at[SENDS.index(send)], recv_sem=recv_sem.at[target],
            device_id=peers[ring][way], device_id_type=MESH,
        )

    def forward(item):
        for send in sends_after(item):
            copy(send).start()

    def relay(items):
        for item in items:
            _, way, hops, k = item
            slot = SLOT[(0, 0, k) if hops == 0 else (way, hops, k)]
            pltpu.make_async_remote_copy(
                src_ref=kv.at[slot], dst_ref=kv.at[slot], send_sem=send_sem.at[0],
                recv_sem=recv_sem.at[slot], device_id=s_up, device_id_type=MESH,
            ).wait_recv()
            forward(item)

    forward(FLAT[0])

    block = lax.broadcasted_iota(jnp.int32, (1, CHUNK), 1) // T
    on = []
    for n in range(CHUNKS):
        row = jnp.zeros((1, CHUNK), F32)
        count = 0
        for j in range(SEVEN):
            ds, df = SHIFT[1 + n * SEVEN + j]
            there = ((s + ds + SIDE) % SIDE) * stride_s + ((f + df + SIDE) % SIDE) * stride_f
            hidden = there >= seq
            row = jnp.where((block == j) & hidden, NEG, row)
            count = count + jnp.where(hidden, 0, 1)
        bias_all[n] = row
        on.append(count)

    for load in rest:
        load.wait()

    def active(ci):
        return sum(jnp.where(ci == n, on[n], 0) for n in range(CHUNKS)) > 0

    k_own = kv[0, pl.ds(0, T), :]
    v_own = kv[0, pl.ds(T, T), :]
    e_own, g_own = feature_pair_t(dot_nt(wk_ref[...], k_own))
    kphi_own = jnp.concatenate([e_own, g_own], axis=0).astype(BF16)
    ones_t = jnp.ones((T, D), BF16)

    row_token = lax.broadcasted_iota(jnp.int32, (PAIR, T), 0)
    row_token = jnp.where(row_token >= T, row_token - T, row_token)
    causal = lax.broadcasted_iota(jnp.int32, (PAIR, T), 1) <= row_token

    prefix[...] = jnp.zeros_like(prefix)
    later[...] = jnp.zeros_like(later)
    own_dphi[...] = jnp.zeros_like(own_dphi)
    loss_acc[...] = jnp.zeros_like(loss_acc)

    def first(j, carry):
        pl.when(j == 2)(functools.partial(relay, FLAT[1:5]))
        pl.when(j == 3)(functools.partial(relay, FLAT[5:9]))
        rows = pl.ds(pl.multiple_of(j * PAIR, PAIR), PAIR)
        q_a = q_ref[:, pl.ds(pl.multiple_of(j * 2 * D, D), D)]
        q_b = q_ref[:, pl.ds(pl.multiple_of(j * 2 * D + D, D), D)]
        q = jnp.concatenate([q_a, q_b], axis=0)
        qs[rows, :] = q
        w = wq_ref[:, pl.ds(pl.multiple_of(j * D, D), D)]
        la, lb = dot(q_a, w), dot(q_b, w)
        plus = lanes(T) < HALF
        xa = jnp.where(plus, la, -pltpu.roll(la, HALF, 1))
        xb = jnp.where(plus, pltpu.roll(lb, HALF, 1), -lb)
        pn = feature_pair(jnp.concatenate([xa, xb], axis=0))
        qpn[rows, :] = pn
        phi = pn.astype(BF16)
        phi_t[j] = phi.T
        q_t[2 * j] = q_a.T
        q_t[2 * j + 1] = q_b.T
        intra = jnp.where(causal, dot(phi, kphi_own), 0.0)
        near_n[rows, :] = dot(intra.astype(BF16), v_own)
        near_d[rows, :] = jnp.broadcast_to(jnp.sum(intra, axis=1, keepdims=True), (PAIR, D))
        scores = jnp.where(causal, dot_nt(q, k_own) * SCALE2, NEG)
        top = jnp.max(scores, axis=1, keepdims=True)
        p = jnp.exp2(scores - top).astype(BF16)
        run_max[rows, :] = jnp.broadcast_to(top, (PAIR, D))
        acc[rows, :] = dot(p, jnp.concatenate([v_own, ones_t], axis=1))

        return carry

    lax.fori_loop(0, TILES, first, 0)

    def chunk_kv(ss):
        blocks = pl.ds(1 + ss * SEVEN, SEVEN)
        k = kv[blocks, pl.ds(0, T), :].reshape(CHUNK, D)
        v = kv[blocks, pl.ds(T, T), :].reshape(CHUNK, D)
        return k, v

    def step(ci, carry):
        for n in range(CHUNKS):
            pl.when(ci == n)(functools.partial(relay, BEFORE[n]))

        live = active(ci)

        @pl.when(jnp.logical_not(live))
        def _():
            kpn[ci] = jnp.zeros((D, CHUNK), F32)

        @pl.when(live)
        def _():
            k, v = chunk_kv(ci)
            v1 = jnp.concatenate([v, jnp.ones((CHUNK, D), BF16)], axis=1)
            bias = bias_all[ci]
            seen = bias == 0.0
            cuts = [(i, min(256, CHUNK - i)) for i in range(0, CHUNK, 256)]

            def score(r):
                rows = pl.ds(r * PAIR, PAIR)
                q = qs[rows, :]
                top = None
                for i, n in cuts:
                    x = dot_nt(q, k[i:i + n]) * SCALE2 + bias[:, i:i + n]
                    scores[r % 2, :, pl.ds(i, n)] = x
                    for c in range(0, n, D):
                        part = x[:, c:c + D]
                        if part.shape[1] < D:
                            fill = jnp.full((PAIR, D - part.shape[1]), NEG, F32)
                            part = jnp.concatenate([part, fill], axis=1)
                        top = part if top is None else jnp.maximum(top, part)
                old = run_max[rows, :]
                new = jnp.maximum(old, jnp.max(top, axis=1, keepdims=True))
                run_max[rows, :] = new
                return new, jnp.exp2(old - new)

            def weigh(r, new, alpha):
                rows = pl.ds(r * PAIR, PAIR)
                for i in range(0, CHUNK, D):
                    n = min(D, CHUNK - i)
                    x = scores[r % 2, :, pl.ds(i, n)]
                    probs[r % 2, :, pl.ds(i, n)] = jnp.exp2(x - new[:, :n]).astype(BF16)
                out = dot(probs[r % 2], v1)
                acc[rows, :] = acc[rows, :] * jnp.concatenate([alpha, alpha], axis=1) + out

            held = score(0)
            e, g = feature_pair_t(dot_nt(wk_ref[...], k))
            pn = jnp.where(seen, jnp.concatenate([e, g], axis=0), 0.0)
            kpn[ci] = pn
            prefix[...] += dot(pn.astype(BF16), v1)
            for r in range(TILES):
                ahead = score(r + 1) if r + 1 < TILES else None
                weigh(r, *held)
                held = ahead

        return carry

    lax.fori_loop(0, CHUNKS, step, 0)

    lane_d = lanes(D)
    norm_hi, norm_lo = hi_lo(prefix[:, D:])
    low[...] = jnp.concatenate(
        [prefix[:, :D], jnp.where(lane_d < HALF, norm_hi, norm_lo)], axis=1
    ).astype(BF16)
    lane = lanes(PAIR)
    lane_t = lanes(T)
    pick_t = jnp.where((lane_t == 0) | (lane_t == HALF), 1.0, 0.0).astype(BF16)
    v_pick = jnp.concatenate([v_own, pick_t], axis=1)

    def exchange(n, source, target, ring):
        me = ring[0][1]

        def make(j):
            return pltpu.make_async_remote_copy(
                src_ref=source(j), dst_ref=target.at[me], send_sem=out_sem.at[n, j],
                recv_sem=in_sem.at[n, me], device_id=ring[j][0], device_id_type=MESH,
            )

        def gather(own):
            total = own
            for j in NEAR:
                slot = ring[j][1]
                pltpu.make_async_remote_copy(
                    src_ref=source(j), dst_ref=target.at[slot], send_sem=out_sem.at[n, j],
                    recv_sem=in_sem.at[n, slot], device_id=ring[j][0], device_id_type=MESH,
                ).wait_recv()
                if own is not None:
                    total = total + target[slot].astype(F32)
            return total

        def begin():
            for j in FAR:
                make(j).start()

        def finished():
            for j in NEAR:
                make(j).wait_send()

        return begin, gather, finished

    def tile_exchange(r):
        return exchange(r, lambda j: parts.at[r, f_ring[j][1]], got1.at[r], f_ring)

    tiles = [tile_exchange(r) for r in range(TILES)]

    def finish(j):
        if j:
            tiles[j - 1][0]()
        rows = pl.ds(pl.multiple_of(j * PAIR, PAIR), PAIR)
        pn = qpn[rows, :]
        phi = pn.astype(BF16)
        far = dot(phi, low[...])
        numer = near_n[rows, :] + far[:, :D]
        far_d = far[:, D:]
        denom = near_d[rows, :] + (far_d + pltpu.roll(far_d, HALF, 1))
        inv = 1.0 / denom
        student = numer * inv
        student_low = student.astype(BF16)
        student_ref[:, pl.ds(pl.multiple_of(j * 2 * D, D), D)] = student_low[:T]
        student_ref[:, pl.ds(pl.multiple_of(j * 2 * D + D, D), D)] = student_low[T:]
        a = acc[rows, :]
        teacher = (a[:, :D] / a[:, D:]).astype(BF16).astype(F32)
        differ = student - teacher
        loss_acc[...] += jnp.sum((differ * differ).reshape(PAIR // 8, 8, D), axis=0)
        grad = differ * (2.0 / TOKENS)
        numer_low = (grad * inv).astype(BF16)
        dg = -jnp.sum(grad * student, axis=1, keepdims=True) * inv
        dg_hi, dg_lo = hi_lo(dg)
        zero = jnp.zeros_like(dg)
        g_key = jnp.where(lane == 0, dg_hi, jnp.where(lane == HALF, dg_lo, zero)).astype(BF16)
        g_later = jnp.where(lane < HALF, dg_hi, dg_lo).astype(BF16)
        g_norm = jnp.where(
            (lane == 0) | (lane == HALF), dg_hi, jnp.where(lane == 1, dg_lo, zero)
        ).astype(BF16)
        coupling = dot_nt(jnp.concatenate([numer_low, g_key], axis=1), v_pick)
        coupling = jnp.where(causal, coupling, 0.0).astype(BF16)
        later[...] += dot(phi_t[j], jnp.concatenate([numer_low, g_later], axis=1))
        own_dphi[...] += dot(phi_t[j], coupling)
        dphi = dot_nt(coupling, kphi_own)
        dphi = dphi + dot_nt(jnp.concatenate([numer_low, g_norm], axis=1), low[...])
        dl = pair_backward(pn, dphi).astype(BF16)
        ga, gb = dot(q_t[2 * j], dl[:T]), dot(q_t[2 * j + 1], dl[T:])
        both = jnp.where(lane_d < HALF, ga, -gb).astype(BF16).reshape(SIDE, 16, D)
        parts[j] = both

    for j in range(TILES):
        finish(j)
    put = pltpu.make_async_copy(student_ref, student_hbm, local_sem.at[5])

    norm = later[:, D:]
    norm_hi, norm_lo = hi_lo(norm + pltpu.roll(norm, HALF, 1))
    low[...] = jnp.concatenate(
        [later[:, :D], jnp.where(lane_d < HALF, norm_hi, norm_lo)], axis=1
    ).astype(BF16)
    tiles[TILES - 1][0]()
    put.start()
    kg_acc[...] = dot(pair_backward_t(e_own, g_own, own_dphi[...]).astype(BF16), k_own)
    lane_c = lanes(CHUNK)
    pick_c = jnp.where((lane_c == 0) | (lane_c == HALF), 1.0, 0.0).astype(BF16)

    def back(ss, carry):
        k, v = chunk_kv(ss)
        d = dot_nt(low[...], jnp.concatenate([v, pick_c], axis=1))
        kg_acc[...] += dot(pair_backward_t(kpn[ss, :HALF], kpn[ss, HALF:], d).astype(BF16), k)
        return carry

    lax.fori_loop(0, CHUNKS, back, 0, unroll=True)
    row = lax.broadcasted_iota(jnp.int32, (8, D), 0)

    def extra(value):
        hi, lo = hi_lo(value)
        return jnp.where(row == 0, hi, jnp.where(row == 1, lo, 0.0))

    def value_of(total):
        return total[8:9, 0:1] + total[9:10, 0:1]

    tail = extra(jnp.sum(loss_acc[...], keepdims=True).reshape(1, 1))
    for i in range(SIDE):
        kparts[i] = jnp.concatenate([kg_acc[pl.ds(8 * i, 8), :], tail], axis=0).astype(BF16)
    k_begin, k_one, k_one_end = exchange(
        4, lambda j: kparts.at[f_ring[j][1]], kgot1, f_ring
    )
    k_begin()
    for send in SENDS:
        copy(send).wait_send()
    for r in range(TILES):
        mid[:, pl.ds(r * D, D)] = tiles[r][1](parts[r, f].astype(F32)).astype(BF16)
    begin, q_two, q_two_end = exchange(5, lambda j: mid, got2, s_ring)
    begin()
    total = k_one(kparts[f].astype(F32))
    kmid[...] = jnp.concatenate([total[:8], extra(value_of(total))], axis=0).astype(BF16)
    begin, k_two, k_two_end = exchange(6, lambda j: kmid, kgot2, s_ring)
    begin()
    for tile in tiles:
        tile[2]()
    k_one_end()
    put.wait()
    full[...] = q_two(mid[...].astype(F32)).astype(BF16)
    begin, q_three, q_three_end = exchange(7, lambda j: full, got3, f_ring)
    begin()
    total = k_two(kmid[...].astype(F32))
    kfull[...] = total.astype(BF16)
    begin, k_three, k_three_end = exchange(8, lambda j: kfull, kgot3, f_ring)
    begin()
    mine[...] = jnp.broadcast_to(value_of(total), (8, D))
    begin, h_one, h_one_end = exchange(9, lambda j: mine, got_loss, h_ring)
    begin()
    got3[f] = full[...]
    kgot3[f] = kfull[...]
    q_two_end()
    k_two_end()
    q_three(None)
    qg_ref[...] = got3[...]
    k_three(None)
    kg_ref[...] = kgot3[...]
    loss_ref[...] = h_one(mine[...])
    for end in (q_three_end, k_three_end, h_one_end):
        end()


def unpack_kernel(student_ref, qg_ref, kg_ref, loss_ref, so_ref, qo_ref, ko_ref, lo_ref):
    so_ref[...] = student_ref[...]
    qo_ref[...] = qg_ref[...].reshape(D, GROUP * HALF).astype(F32)
    for i in range(SIDE):
        ko_ref[pl.ds(8 * i, 8), :] = kg_ref[i].astype(F32)[:8]
    lo_ref[...] = loss_ref[0:1, 0:1] * (1.0 / TOKENS)


def attend(queries, key_matrix, value_matrix, query_feature_weight, key_feature_weight):
    vmem = pl.BlockSpec(memory_space=pltpu.VMEM)
    anywhere = pl.BlockSpec(memory_space=pl.ANY)
    dma = pltpu.SemaphoreType.DMA
    one, all_of = (16,), (SIDE, 16)
    exchanges = (all_of, all_of, one, all_of, one, all_of)
    return pl.pallas_call(
        main_kernel,
        out_shape=(
            jax.ShapeDtypeStruct((T, GROUP * D), BF16),
            jax.ShapeDtypeStruct((SIDE, 16, GROUP * HALF), BF16),
            jax.ShapeDtypeStruct((SIDE, 16, D), BF16),
            jax.ShapeDtypeStruct((8, D), F32),
        ),
        in_specs=[anywhere] * 5,
        out_specs=(anywhere, vmem, vmem, vmem),
        scratch_shapes=[
            pltpu.VMEM((BLOCKS, 2 * T, D), BF16),
            pltpu.VMEM((ROWS, D), BF16),
            pltpu.VMEM((ROWS, D), F32),
            pltpu.VMEM((CHUNKS, D, CHUNK), F32),
            pltpu.VMEM((ROWS, D), F32),
            pltpu.VMEM((ROWS, 2 * D), F32),
            pltpu.VMEM((2, PAIR, CHUNK), F32),
            pltpu.VMEM((2, PAIR, CHUNK), BF16),
            pltpu.VMEM((CHUNKS, 1, CHUNK), F32),
            pltpu.VMEM((D, 2 * D), F32),
            pltpu.VMEM((D, 2 * D), F32),
            pltpu.VMEM((D, 2 * D), BF16),
            pltpu.VMEM((D, T), F32),
            pltpu.VMEM((8, D), F32),
            pltpu.VMEM((HALF, D), F32),
        ]
        + [pltpu.VMEM((TILES,) + all_of + (D,), BF16)] * 2
        + [pltpu.VMEM(shape + (512,), BF16) for shape in exchanges[2:]]
        + [pltpu.VMEM(shape + (D,), BF16) for shape in exchanges]
        + [
            pltpu.VMEM((8, D), F32),
            pltpu.VMEM((SIDE, 8, D), F32),
            pltpu.VMEM((TILES, D, PAIR), BF16),
            pltpu.VMEM((GROUP, D, T), BF16),
            pltpu.VMEM((ROWS, D), F32),
            pltpu.VMEM((ROWS, D), F32),
            pltpu.VMEM((T, GROUP * D), BF16),
            pltpu.VMEM((D, GROUP * HALF), BF16),
            pltpu.VMEM((HALF, D), BF16),
            pltpu.VMEM((T, GROUP * D), BF16),
            dma((6,)),
            dma((BLOCKS,)),
            dma((len(SENDS),)),
            dma((10, SIDE)),
            dma((10, SIDE)),
        ],
        compiler_params=pltpu.CompilerParams(
            collective_id=0, has_side_effects=True, vmem_limit_bytes=56 * 1024 * 1024
        ),
        name="attend",
    )(queries, key_matrix, value_matrix, query_feature_weight, key_feature_weight.T)


def unpack(*operands):
    vmem = pl.BlockSpec(memory_space=pltpu.VMEM)
    return pl.pallas_call(
        unpack_kernel,
        out_shape=(
            jax.ShapeDtypeStruct((T, GROUP * D), BF16),
            jax.ShapeDtypeStruct((D, GROUP * HALF), F32),
            jax.ShapeDtypeStruct((HALF, D), F32),
            jax.ShapeDtypeStruct((1, 1), F32),
        ),
        in_specs=[vmem] * 4,
        out_specs=(vmem,) * 4,
        name="unpack",
    )(*operands)


def local(*operands):
    student, qo, ko, lo = unpack(*attend(*operands))
    return student, qo, ko.T, lo.reshape(())


def solution(mesh):
    placed = (
        P("seq", "head"),
        P("seq", "head"),
        P("seq", "head"),
        P(None, "head"),
        P(None, "head"),
    )
    return jax.shard_map(
        local,
        mesh=mesh,
        in_specs=placed,
        out_specs=(P("seq", "head"), P(None, "head"), P(None, "head"), P()),
        check_vma=False,
    )
```

```python
import functools

import jax
import jax.numpy as jnp
from jax import lax
from jax.experimental import pallas as pl
from jax.experimental.pallas import tpu as pltpu
from jax.sharding import PartitionSpec as P

D = 128
GROUP = 8
HALF = 64
T = 144
SIDE = 8
BLOCKS = SIDE * SIDE
TOKENS = BLOCKS * T
SEVEN = 7
CHUNKS = 9
CHUNK = SEVEN * T
ROWS = GROUP * T
PAIR = 2 * T
TILES = ROWS // PAIR
NEG = -1e30
SCALE2 = (D ** -0.5) * 1.4426950408889634
MESH = pl.DeviceIdType.MESH
F32 = jnp.float32
BF16 = jnp.bfloat16


def dot(a, b):
    return lax.dot_general(a, b, (((1,), (0,)), ((), ())), preferred_element_type=F32)


def dot_nt(a, b):
    return lax.dot_general(a, b, (((1,), (1,)), ((), ())), preferred_element_type=F32)


def dot_tn(a, b):
    return lax.dot_general(a, b, (((0,), (0,)), ((), ())), preferred_element_type=F32)


def lanes(rows):
    return lax.broadcasted_iota(jnp.int32, (rows, D), 1)


def halves(x, reduce, neutral):
    plus = lanes(x.shape[0]) < HALF
    a = reduce(jnp.where(plus, x, neutral), axis=1, keepdims=True)
    b = reduce(jnp.where(plus, neutral, x), axis=1, keepdims=True)
    return a, b, plus


def feature_pair(x):
    a, b, plus = halves(x, jnp.max, -jnp.inf)
    e = jnp.exp(x - jnp.where(plus, a, b))
    sa, sb, _ = halves(e, jnp.sum, 0.0)
    return e * jnp.where(plus, 1.0 / sa, 1.0 / sb)


def pair_backward(pn, d):
    a, b, plus = halves(pn * d, jnp.sum, 0.0)
    t = pn * (d - jnp.where(plus, a, b))
    return t - pltpu.roll(t, HALF, 1)


def feature_pair_t(x):
    a = jnp.max(x, axis=0, keepdims=True)
    b = jnp.min(x, axis=0, keepdims=True)
    e, g = jnp.exp(x - a), jnp.exp(b - x)
    e = e * (1.0 / jnp.sum(e, axis=0, keepdims=True))
    g = g * (1.0 / jnp.sum(g, axis=0, keepdims=True))
    return e, g


def pair_backward_t(e, g, d):
    dp, dn = d[:HALF], d[HALF:]
    a = jnp.sum(e * dp, axis=0, keepdims=True)
    b = jnp.sum(g * dn, axis=0, keepdims=True)
    return e * (dp - a) - g * (dn - b)


def hi_lo(x):
    hi = x.astype(BF16).astype(F32)
    return hi, x - hi


def place():
    seq = lax.axis_index("seq")
    head = lax.axis_index("head")
    core = head % 2
    y, z = seq % SIDE, seq // SIDE
    f = y + core * (z - y)
    s = z + core * (y - z)
    stride_f = 1 + (SIDE - 1) * core
    stride_s = SIDE - (SIDE - 1) * core
    return seq, head, f, s, stride_f, stride_s


def offset(k):
    return k // 2 - (k % 2) * k


FAR = (4, 3, 5, 2, 6, 1, 7)
NEAR = FAR[::-1]


ARRIVAL = (
    0, 10, 1, 110, 2, 20, 3, 111, 4, 11, 120, 12, 112, 30, 5, 113,
    6, 13, 121, 14, 114, 130, 21, 122, 7, 22, 115, 40, 123, 15, 116, 16,
    131, 23, 124, 24, 132, 31, 117, 17, 125, 32, 133, 25, 126, 26, 134, 33,
    127, 34, 135, 41, 136, 27, 144, 42, 137, 35, 145, 36, 146, 43, 147, 37,
)


def unpacked(code):
    way, hops, k = code // 100, code // 10 % 10, code % 10
    if hops:
        return ("s", way, hops, k)
    return ("own", 0, 0, 0) if k == 0 else ("f", 1 - k % 2, 0, k)


FLAT = [unpacked(code) for code in ARRIVAL]
SLOT = {}
SHIFT = []
for ring, way, hops, k in FLAT:
    SLOT[(0, 0, k) if hops == 0 else (way, hops, k)] = len(SHIFT)
    SHIFT.append((-hops if way == 0 else hops, offset(k)) if hops else (0, offset(k)))
CUTS = (9, 12, 21, 29, 35, 41, 47, 53, 59, 64)
BEFORE = [FLAT[a:b] for a, b in zip(CUTS, CUTS[1:])]


def sends_after(item):
    ring, way, hops, k = item
    out = []
    if hops == 0:
        mine = SLOT[(0, 0, k)]
        far = abs(offset(k))
        for step in (0, 1):
            if (ring == "own" or step == way) and far < (4 if step == 0 else 3):
                there = SLOT[(0, 0, 2 * (far + 1) - 1 if step == 0 else 2 * (far + 1))]
                out.append((mine, there, 0, step))
        for step in (0, 1):
            out.append((mine, SLOT[(step, 1, k)], 1, step))
    else:
        there = (way, hops + 1, k)
        if there in SLOT:
            out.append((SLOT[(way, hops, k)], SLOT[there], 1, way))
    return out


SENDS = [send for item in FLAT for send in sends_after(item)]


def main_kernel(
    q_hbm, k_hbm, v_hbm, wq_hbm, wk_hbm,
    student_hbm, qg_ref, kg_ref, loss_ref,
    kv, qs, qpn, kpn, run_max, acc, scores, probs, bias_all, prefix, later, low, own_dphi, loss_acc, kg_acc,
    parts, got1, mid, got2, full, got3, kparts, kgot1, kmid, kgot2, kfull, kgot3, mine, got_loss,
    phi_t, q_t, near_n, near_d, q_ref, wq_ref, wk_ref, student_ref,
    local_sem, recv_sem, send_sem, out_sem, in_sem,
):
    seq, head, f, s, stride_f, stride_s = place()

    def rank(ff, ss):
        return (ff * stride_f + ss * stride_s, head)

    f_up, f_dn = rank((f + 1) % SIDE, s), rank((f + SIDE - 1) % SIDE, s)
    s_up, s_dn = rank(f, (s + 1) % SIDE), rank(f, (s + SIDE - 1) % SIDE)

    load_k = pltpu.make_async_copy(k_hbm, kv.at[0, pl.ds(0, T)], local_sem.at[0])
    load_v = pltpu.make_async_copy(v_hbm, kv.at[0, pl.ds(T, T)], local_sem.at[1])
    load_k.start()
    load_v.start()
    rest = [
        pltpu.make_async_copy(source, target, local_sem.at[n])
        for n, source, target in ((2, wk_hbm, wk_ref), (3, q_hbm, q_ref), (4, wq_hbm, wq_ref))
    ]
    for load in rest:
        load.start()
    def f_rank(j):
        return rank((f + j) % SIDE, s)

    def s_rank(j):
        return rank(f, (s + j) % SIDE)

    def h_rank(j):
        return (seq, (head + j) % SIDE)

    barrier = pltpu.get_barrier_semaphore()
    f_ring = [(None, f)] + [(f_rank(j), (f + j) % SIDE) for j in range(1, SIDE)]
    s_ring = [(None, s)] + [(s_rank(j), (s + j) % SIDE) for j in range(1, SIDE)]
    h_ring = [(None, head)] + [(h_rank(j), (head + j) % SIDE) for j in range(1, SIDE)]
    for ring in (f_ring, s_ring, h_ring):
        for peer, _ in ring[1:]:
            pl.semaphore_signal(barrier, inc=1, device_id=peer, device_id_type=MESH)
    load_k.wait()
    load_v.wait()
    pl.semaphore_wait(barrier, 3 * (SIDE - 1))

    peers = ((f_up, f_dn), (s_up, s_dn))

    def copy(send):
        source, target, ring, way = send
        return pltpu.make_async_remote_copy(
            src_ref=kv.at[source], dst_ref=kv.at[target],
            send_sem=send_sem.at[SENDS.index(send)], recv_sem=recv_sem.at[target],
            device_id=peers[ring][way], device_id_type=MESH,
        )

    def forward(item):
        for send in sends_after(item):
            copy(send).start()

    def relay(items):
        for item in items:
            _, way, hops, k = item
            slot = SLOT[(0, 0, k) if hops == 0 else (way, hops, k)]
            pltpu.make_async_remote_copy(
                src_ref=kv.at[slot], dst_ref=kv.at[slot], send_sem=send_sem.at[0],
                recv_sem=recv_sem.at[slot], device_id=s_up, device_id_type=MESH,
            ).wait_recv()
            forward(item)

    forward(FLAT[0])

    block = lax.broadcasted_iota(jnp.int32, (1, CHUNK), 1) // T
    on = []
    for n in range(CHUNKS):
        row = jnp.zeros((1, CHUNK), F32)
        count = 0
        for j in range(SEVEN):
            ds, df = SHIFT[1 + n * SEVEN + j]
            there = ((s + ds + SIDE) % SIDE) * stride_s + ((f + df + SIDE) % SIDE) * stride_f
            hidden = there >= seq
            row = jnp.where((block == j) & hidden, NEG, row)
            count = count + jnp.where(hidden, 0, 1)
        bias_all[n] = row
        on.append(count)

    for load in rest:
        load.wait()

    def active(ci):
        return sum(jnp.where(ci == n, on[n], 0) for n in range(CHUNKS)) > 0

    k_own = kv[0, pl.ds(0, T), :]
    v_own = kv[0, pl.ds(T, T), :]
    e_own, g_own = feature_pair_t(dot_nt(wk_ref[...], k_own))
    kphi_own = jnp.concatenate([e_own, g_own], axis=0).astype(BF16)
    ones_t = jnp.ones((T, D), BF16)

    row_token = lax.broadcasted_iota(jnp.int32, (PAIR, T), 0)
    row_token = jnp.where(row_token >= T, row_token - T, row_token)
    causal = lax.broadcasted_iota(jnp.int32, (PAIR, T), 1) <= row_token

    prefix[...] = jnp.zeros_like(prefix)
    later[...] = jnp.zeros_like(later)
    own_dphi[...] = jnp.zeros_like(own_dphi)
    loss_acc[...] = jnp.zeros_like(loss_acc)

    def first(j, carry):
        pl.when(j == 2)(functools.partial(relay, FLAT[1:5]))
        pl.when(j == 3)(functools.partial(relay, FLAT[5:9]))
        rows = pl.ds(pl.multiple_of(j * PAIR, PAIR), PAIR)
        q_a = q_ref[:, pl.ds(pl.multiple_of(j * 2 * D, D), D)]
        q_b = q_ref[:, pl.ds(pl.multiple_of(j * 2 * D + D, D), D)]
        q = jnp.concatenate([q_a, q_b], axis=0)
        qs[rows, :] = q
        w = wq_ref[:, pl.ds(pl.multiple_of(j * D, D), D)]
        la, lb = dot(q_a, w), dot(q_b, w)
        plus = lanes(T) < HALF
        xa = jnp.where(plus, la, -pltpu.roll(la, HALF, 1))
        xb = jnp.where(plus, pltpu.roll(lb, HALF, 1), -lb)
        pn = feature_pair(jnp.concatenate([xa, xb], axis=0))
        qpn[rows, :] = pn
        phi = pn.astype(BF16)
        phi_t[j] = phi.T
        q_t[2 * j] = q_a.T
        q_t[2 * j + 1] = q_b.T
        intra = jnp.where(causal, dot(phi, kphi_own), 0.0)
        near_n[rows, :] = dot(intra.astype(BF16), v_own)
        near_d[rows, :] = jnp.broadcast_to(jnp.sum(intra, axis=1, keepdims=True), (PAIR, D))
        scores = jnp.where(causal, dot_nt(q, k_own) * SCALE2, NEG)
        top = jnp.max(scores, axis=1, keepdims=True)
        p = jnp.exp2(scores - top).astype(BF16)
        run_max[rows, :] = jnp.broadcast_to(top, (PAIR, D))
        acc[rows, :] = dot(p, jnp.concatenate([v_own, ones_t], axis=1))

        return carry

    lax.fori_loop(0, TILES, first, 0)

    def chunk_kv(ss):
        blocks = pl.ds(1 + ss * SEVEN, SEVEN)
        k = kv[blocks, pl.ds(0, T), :].reshape(CHUNK, D)
        v = kv[blocks, pl.ds(T, T), :].reshape(CHUNK, D)
        return k, v

    def step(ci, carry):
        for n in range(CHUNKS):
            pl.when(ci == n)(functools.partial(relay, BEFORE[n]))

        live = active(ci)

        @pl.when(jnp.logical_not(live))
        def _():
            kpn[ci] = jnp.zeros((D, CHUNK), F32)

        @pl.when(live)
        def _():
            k, v = chunk_kv(ci)
            v1 = jnp.concatenate([v, jnp.ones((CHUNK, D), BF16)], axis=1)
            bias = bias_all[ci]
            seen = bias == 0.0
            cuts = [(i, min(256, CHUNK - i)) for i in range(0, CHUNK, 256)]

            def score(r):
                rows = pl.ds(r * PAIR, PAIR)
                q = qs[rows, :]
                top = None
                for i, n in cuts:
                    x = dot_nt(q, k[i:i + n]) * SCALE2 + bias[:, i:i + n]
                    scores[r % 2, :, pl.ds(i, n)] = x
                    for c in range(0, n, D):
                        part = x[:, c:c + D]
                        if part.shape[1] < D:
                            fill = jnp.full((PAIR, D - part.shape[1]), NEG, F32)
                            part = jnp.concatenate([part, fill], axis=1)
                        top = part if top is None else jnp.maximum(top, part)
                old = run_max[rows, :]
                new = jnp.maximum(old, jnp.max(top, axis=1, keepdims=True))
                run_max[rows, :] = new
                return new, jnp.exp2(old - new)

            def weigh(r, new, alpha):
                rows = pl.ds(r * PAIR, PAIR)
                for i in range(0, CHUNK, D):
                    n = min(D, CHUNK - i)
                    x = scores[r % 2, :, pl.ds(i, n)]
                    probs[r % 2, :, pl.ds(i, n)] = jnp.exp2(x - new[:, :n]).astype(BF16)
                out = dot(probs[r % 2], v1)
                acc[rows, :] = acc[rows, :] * jnp.concatenate([alpha, alpha], axis=1) + out

            held = score(0)
            e, g = feature_pair_t(dot_nt(wk_ref[...], k))
            pn = jnp.where(seen, jnp.concatenate([e, g], axis=0), 0.0)
            kpn[ci] = pn
            prefix[...] += dot(pn.astype(BF16), v1)
            for r in range(TILES):
                ahead = score(r + 1) if r + 1 < TILES else None
                weigh(r, *held)
                held = ahead

        return carry

    lax.fori_loop(0, CHUNKS, step, 0)

    lane_d = lanes(D)
    norm_hi, norm_lo = hi_lo(prefix[:, D:])
    low[...] = jnp.concatenate(
        [prefix[:, :D], jnp.where(lane_d < HALF, norm_hi, norm_lo)], axis=1
    ).astype(BF16)
    lane = lanes(PAIR)
    lane_t = lanes(T)
    pick_t = jnp.where((lane_t == 0) | (lane_t == HALF), 1.0, 0.0).astype(BF16)
    v_pick = jnp.concatenate([v_own, pick_t], axis=1)

    def exchange(n, source, target, ring):
        me = ring[0][1]

        def make(j):
            return pltpu.make_async_remote_copy(
                src_ref=source(j), dst_ref=target.at[me], send_sem=out_sem.at[n, j],
                recv_sem=in_sem.at[n, me], device_id=ring[j][0], device_id_type=MESH,
            )

        def gather(own):
            total = own
            for j in NEAR:
                slot = ring[j][1]
                pltpu.make_async_remote_copy(
                    src_ref=source(j), dst_ref=target.at[slot], send_sem=out_sem.at[n, j],
                    recv_sem=in_sem.at[n, slot], device_id=ring[j][0], device_id_type=MESH,
                ).wait_recv()
                if own is not None:
                    total = total + target[slot].astype(F32)
            return total

        def begin():
            for j in FAR:
                make(j).start()

        def finished():
            for j in NEAR:
                make(j).wait_send()

        return begin, gather, finished

    def tile_exchange(r):
        return exchange(r, lambda j: parts.at[r, f_ring[j][1]], got1.at[r], f_ring)

    tiles = [tile_exchange(r) for r in range(TILES)]

    def finish(j):
        if j:
            tiles[j - 1][0]()
        rows = pl.ds(pl.multiple_of(j * PAIR, PAIR), PAIR)
        pn = qpn[rows, :]
        phi = pn.astype(BF16)
        far = dot(phi, low[...])
        numer = near_n[rows, :] + far[:, :D]
        far_d = far[:, D:]
        denom = near_d[rows, :] + (far_d + pltpu.roll(far_d, HALF, 1))
        inv = 1.0 / denom
        student = numer * inv
        student_low = student.astype(BF16)
        student_ref[:, pl.ds(pl.multiple_of(j * 2 * D, D), D)] = student_low[:T]
        student_ref[:, pl.ds(pl.multiple_of(j * 2 * D + D, D), D)] = student_low[T:]
        a = acc[rows, :]
        teacher = (a[:, :D] / a[:, D:]).astype(BF16).astype(F32)
        differ = student - teacher
        loss_acc[...] += jnp.sum((differ * differ).reshape(PAIR // 8, 8, D), axis=0)
        grad = differ * (2.0 / TOKENS)
        numer_low = (grad * inv).astype(BF16)
        dg = -jnp.sum(grad * student, axis=1, keepdims=True) * inv
        dg_hi, dg_lo = hi_lo(dg)
        zero = jnp.zeros_like(dg)
        g_key = jnp.where(lane == 0, dg_hi, jnp.where(lane == HALF, dg_lo, zero)).astype(BF16)
        g_later = jnp.where(lane < HALF, dg_hi, dg_lo).astype(BF16)
        g_norm = jnp.where(
            (lane == 0) | (lane == HALF), dg_hi, jnp.where(lane == 1, dg_lo, zero)
        ).astype(BF16)
        coupling = dot_nt(jnp.concatenate([numer_low, g_key], axis=1), v_pick)
        coupling = jnp.where(causal, coupling, 0.0).astype(BF16)
        later[...] += dot(phi_t[j], jnp.concatenate([numer_low, g_later], axis=1))
        own_dphi[...] += dot(phi_t[j], coupling)
        dphi = dot_nt(coupling, kphi_own)
        dphi = dphi + dot_nt(jnp.concatenate([numer_low, g_norm], axis=1), low[...])
        dl = pair_backward(pn, dphi).astype(BF16)
        ga, gb = dot(q_t[2 * j], dl[:T]), dot(q_t[2 * j + 1], dl[T:])
        both = jnp.where(lane_d < HALF, ga, -gb).astype(BF16).reshape(SIDE, 16, D)
        parts[j] = both

    for j in range(TILES):
        finish(j)
    put = pltpu.make_async_copy(student_ref, student_hbm, local_sem.at[5])

    norm = later[:, D:]
    norm_hi, norm_lo = hi_lo(norm + pltpu.roll(norm, HALF, 1))
    low[...] = jnp.concatenate(
        [later[:, :D], jnp.where(lane_d < HALF, norm_hi, norm_lo)], axis=1
    ).astype(BF16)
    tiles[TILES - 1][0]()
    put.start()
    kg_acc[...] = dot(pair_backward_t(e_own, g_own, own_dphi[...]).astype(BF16), k_own)
    lane_c = lanes(CHUNK)
    pick_c = jnp.where((lane_c == 0) | (lane_c == HALF), 1.0, 0.0).astype(BF16)

    def back(ss, carry):
        k, v = chunk_kv(ss)
        d = dot_nt(low[...], jnp.concatenate([v, pick_c], axis=1))
        kg_acc[...] += dot(pair_backward_t(kpn[ss, :HALF], kpn[ss, HALF:], d).astype(BF16), k)
        return carry

    lax.fori_loop(0, CHUNKS, back, 0, unroll=True)
    row = lax.broadcasted_iota(jnp.int32, (8, D), 0)

    def extra(value):
        hi, lo = hi_lo(value)
        return jnp.where(row == 0, hi, jnp.where(row == 1, lo, 0.0))

    def value_of(total):
        return total[8:9, 0:1] + total[9:10, 0:1]

    tail = extra(jnp.sum(loss_acc[...], keepdims=True).reshape(1, 1))
    for i in range(SIDE):
        kparts[i] = jnp.concatenate([kg_acc[pl.ds(8 * i, 8), :], tail], axis=0).astype(BF16)
    k_begin, k_one, k_one_end = exchange(
        4, lambda j: kparts.at[f_ring[j][1]], kgot1, f_ring
    )
    k_begin()
    for send in SENDS:
        copy(send).wait_send()
    twos = [exchange(10 + i, lambda j, i=i: mid.at[i], got2.at[i], s_ring) for i in range(2)]
    threes = [exchange(12 + i, lambda j, i=i: full.at[i], got3.at[i], f_ring) for i in range(2)]
    for r in range(TILES):
        mid[r // 2, :, pl.ds(r % 2 * D, D)] = tiles[r][1](parts[r, f].astype(F32)).astype(BF16)
        if r % 2:
            twos[r // 2][0]()
    total = k_one(kparts[f].astype(F32))
    kmid[...] = jnp.concatenate([total[:8], extra(value_of(total))], axis=0).astype(BF16)
    begin, k_two, k_two_end = exchange(6, lambda j: kmid, kgot2, s_ring)
    begin()
    for tile in tiles:
        tile[2]()
    k_one_end()
    put.wait()
    for i in range(2):
        full[i] = twos[i][1](mid[i].astype(F32)).astype(BF16)
        threes[i][0]()
    total = k_two(kmid[...].astype(F32))
    kfull[...] = total.astype(BF16)
    begin, k_three, k_three_end = exchange(8, lambda j: kfull, kgot3, f_ring)
    begin()
    mine[...] = jnp.broadcast_to(value_of(total), (8, D))
    begin, h_one, h_one_end = exchange(9, lambda j: mine, got_loss, h_ring)
    begin()
    for i in range(2):
        got3[i, f] = full[i]
    kgot3[f] = kfull[...]
    for two in twos:
        two[2]()
    k_two_end()
    for i in range(2):
        threes[i][1](None)
        qg_ref[i] = got3[i]
    k_three(None)
    kg_ref[...] = kgot3[...]
    loss_ref[...] = h_one(mine[...])
    for end in (threes[0][2], threes[1][2], k_three_end, h_one_end):
        end()


def unpack_kernel(student_ref, qg_ref, kg_ref, loss_ref, so_ref, qo_ref, ko_ref, lo_ref):
    so_ref[...] = student_ref[...]
    for i in range(2):
        qo_ref[:, pl.ds(i * 2 * D, 2 * D)] = qg_ref[i].reshape(D, 2 * D).astype(F32)
    for i in range(SIDE):
        ko_ref[pl.ds(8 * i, 8), :] = kg_ref[i].astype(F32)[:8]
    lo_ref[...] = loss_ref[0:1, 0:1] * (1.0 / TOKENS)


def attend(queries, key_matrix, value_matrix, query_feature_weight, key_feature_weight):
    vmem = pl.BlockSpec(memory_space=pltpu.VMEM)
    anywhere = pl.BlockSpec(memory_space=pl.ANY)
    dma = pltpu.SemaphoreType.DMA
    one, all_of = (16,), (SIDE, 16)
    exchanges = (all_of, all_of, one, all_of, one, all_of)
    return pl.pallas_call(
        main_kernel,
        out_shape=(
            jax.ShapeDtypeStruct((T, GROUP * D), BF16),
            jax.ShapeDtypeStruct((2, SIDE, 16, 2 * D), BF16),
            jax.ShapeDtypeStruct((SIDE, 16, D), BF16),
            jax.ShapeDtypeStruct((8, D), F32),
        ),
        in_specs=[anywhere] * 5,
        out_specs=(anywhere, vmem, vmem, vmem),
        scratch_shapes=[
            pltpu.VMEM((BLOCKS, 2 * T, D), BF16),
            pltpu.VMEM((ROWS, D), BF16),
            pltpu.VMEM((ROWS, D), F32),
            pltpu.VMEM((CHUNKS, D, CHUNK), F32),
            pltpu.VMEM((ROWS, D), F32),
            pltpu.VMEM((ROWS, 2 * D), F32),
            pltpu.VMEM((2, PAIR, CHUNK), F32),
            pltpu.VMEM((2, PAIR, CHUNK), BF16),
            pltpu.VMEM((CHUNKS, 1, CHUNK), F32),
            pltpu.VMEM((D, 2 * D), F32),
            pltpu.VMEM((D, 2 * D), F32),
            pltpu.VMEM((D, 2 * D), BF16),
            pltpu.VMEM((D, T), F32),
            pltpu.VMEM((8, D), F32),
            pltpu.VMEM((HALF, D), F32),
        ]
        + [pltpu.VMEM((TILES,) + all_of + (D,), BF16)] * 2
        + [pltpu.VMEM((2,) + shape + (2 * D,), BF16) for shape in exchanges[2:]]
        + [pltpu.VMEM(shape + (D,), BF16) for shape in exchanges]
        + [
            pltpu.VMEM((8, D), F32),
            pltpu.VMEM((SIDE, 8, D), F32),
            pltpu.VMEM((TILES, D, PAIR), BF16),
            pltpu.VMEM((GROUP, D, T), BF16),
            pltpu.VMEM((ROWS, D), F32),
            pltpu.VMEM((ROWS, D), F32),
            pltpu.VMEM((T, GROUP * D), BF16),
            pltpu.VMEM((D, GROUP * HALF), BF16),
            pltpu.VMEM((HALF, D), BF16),
            pltpu.VMEM((T, GROUP * D), BF16),
            dma((6,)),
            dma((BLOCKS,)),
            dma((len(SENDS),)),
            dma((14, SIDE)),
            dma((14, SIDE)),
        ],
        compiler_params=pltpu.CompilerParams(
            collective_id=0, has_side_effects=True, vmem_limit_bytes=56 * 1024 * 1024
        ),
        name="attend",
    )(queries, key_matrix, value_matrix, query_feature_weight, key_feature_weight.T)


def unpack(*operands):
    vmem = pl.BlockSpec(memory_space=pltpu.VMEM)
    return pl.pallas_call(
        unpack_kernel,
        out_shape=(
            jax.ShapeDtypeStruct((T, GROUP * D), BF16),
            jax.ShapeDtypeStruct((D, GROUP * HALF), F32),
            jax.ShapeDtypeStruct((HALF, D), F32),
            jax.ShapeDtypeStruct((1, 1), F32),
        ),
        in_specs=[vmem] * 4,
        out_specs=(vmem,) * 4,
        name="unpack",
    )(*operands)


def local(*operands):
    student, qo, ko, lo = unpack(*attend(*operands))
    return student, qo, ko.T, lo.reshape(())


def solution(mesh):
    placed = (
        P("seq", "head"),
        P("seq", "head"),
        P("seq", "head"),
        P(None, "head"),
        P(None, "head"),
    )
    return jax.shard_map(
        local,
        mesh=mesh,
        in_specs=placed,
        out_specs=(P("seq", "head"), P(None, "head"), P(None, "head"), P()),
        check_vma=False,
    )
```
